128 devices in a mesh: tm: 16 (over y, x), head: 8 (over z, core).
Axes of the slice: x: 4, y: 4, z: 4, core: 2. Of those that a mesh axis runs over, the one named last changes fastest.
Arguments:
- inputs: bfloat16 [8192, 2048], P('tm', 'head'), may hold values from -6 to 6
- in_weight: bfloat16 [2048, 2048], P(None, 'head'), may hold values from -0.00036621094 to 0.00036621094
- rec_weight: float32 [16, 128, 128], P('head'), may hold values from -1 to 1, as said below
- bias: float32 [2048], P('head'), may hold values from -0.0012207031 to 0.0012207031
- initial: float32 [2048], P('head'), may hold values from -0.25 to 0.25
- guess: float32 [8192, 2048], P('tm', 'head'), may hold values from -0.25 to 0.25
Outputs:
- trajectory: float32 [8192, 2048], P('tm', 'head')
- next_guess: float32 [8192, 2048], P('tm', 'head')
The draws below stay inside these ranges and needn't reach their ends.
Inputs may be any that keep to these rules, and one draw needn't show every extreme that they name: `rec_weight`: each head's matrix has operator norm below one.
All inputs are finite; a program needn't handle non-finite values.
Results may differ from the reference program's by a relative error of at most 0.0003.
Values may be sent and summed in bfloat16 or wider, within the bound.
A program may use at most 128 MiB of HBM per device.

```python
import math
import jax
import jax.numpy as jnp
from jax import lax

HEADS = 16
HEAD_SIZE = 128
SLAB = 512
SWEEPS = 2
D = 2048
WINDOW = 8192


def draw_rec_weight(key, part):
    kind_key, rate_key, spread_key, noise_key = jax.random.split(jax.random.fold_in(key, 17), 4)
    fast_share = 0.35
    slow_low, slow_high = (0.1, 1.0)
    noise = jax.random.normal(noise_key, (HEADS, HEAD_SIZE, HEAD_SIZE), jnp.float32)
    is_fast = jax.random.uniform(kind_key, (HEADS,), jnp.float32) < fast_share
    pick = jax.random.uniform(rate_key, (HEADS,), jnp.float32)
    slow_decay = jnp.exp(math.log(slow_low) + pick * (math.log(slow_high) - math.log(slow_low))) / SLAB
    fast_decay = jnp.exp(math.log(1.0 / 50.0) + pick * (math.log(1.0 / 30.0) - math.log(1.0 / 50.0)))
    decay = jnp.where(is_fast, fast_decay, slow_decay)
    spread = jax.random.uniform(spread_key, (HEADS, HEAD_SIZE), jnp.float32, 0.7, 1.3)
    rates = jnp.exp(-decay[:, None] * spread)
    noise = jnp.clip(noise, -3.0, 3.0) * (0.4 / math.sqrt(HEAD_SIZE))
    identity = jnp.eye(HEAD_SIZE, dtype=jnp.float32)
    start = (identity[None, :, :] + noise) / 1.8

    def refine(counter, matrix):
        square = jnp.einsum('hij,hkj->hik', matrix, matrix, precision=lax.Precision.HIGHEST)
        cubic = jnp.einsum('hik,hkj->hij', square, matrix, precision=lax.Precision.HIGHEST)
        return 1.5 * matrix - 0.5 * cubic
    rotation = lax.fori_loop(0, 30, refine, start)
    root = jnp.sqrt(rates)
    return root[:, :, None] * rotation * root[:, None, :]


def block_levels(own_key, dims, cuts, smallest, largest):
    def one(position, parts):
        steps = jax.random.uniform(jax.random.fold_in(jax.random.fold_in(own_key, 6), position), (parts,), jnp.float32, smallest / len(cuts), largest / len(cuts))
        return jnp.repeat(jnp.exp(steps), dims[position] // parts).reshape((-1,) + (1,) * (len(dims) - position - 1))

    level = one(*cuts[0])
    for cut in cuts[1:]:
        level = level * one(*cut)
    return level


def gaussian(stream_key, extent, scale, bound, cuts=(), kind=jnp.bfloat16):
    result = scale * jax.random.normal(stream_key, extent, jnp.float32)
    if cuts:
        result = result * block_levels(stream_key, extent, cuts, -0.22, 0.18)
    return jnp.clip(result, -bound, bound).astype(kind)


def setup_inputs(seed: int = 0) -> dict:
    seeds = jax.random.split(jax.random.key(seed), 7)
    inputs = gaussian(seeds[0], (WINDOW, D), 1.0, 6.0, ((0, 16), (1, 8)))
    in_weight = gaussian(seeds[1], (D, D), (D * SLAB * SLAB // 2) ** -0.5, 0.00036621094, ((1, 8),))
    rec_weight = draw_rec_weight(jax.random.fold_in(seeds[6], 71), 0)
    bias = gaussian(seeds[3], (D,), (100 * SLAB * SLAB) ** -0.5, 0.0012207031, ((0, 8),), jnp.float32)
    initial = gaussian(seeds[4], (D,), SLAB ** -0.5, 0.25, ((0, 8),), jnp.float32)
    guess = gaussian(seeds[5], (WINDOW, D), SLAB ** -0.5, 0.25, ((0, 16), (1, 8)), jnp.float32)
    return dict(inputs=inputs, in_weight=in_weight, rec_weight=rec_weight, bias=bias, initial=initial, guess=guess)


def reference(inputs, in_weight, rec_weight, bias, initial, guess):
    total = inputs.shape[0]
    drive = jnp.dot(inputs, in_weight, preferred_element_type=jnp.float32) + bias
    drive = drive.reshape(total, HEADS, HEAD_SIZE)
    start_state = initial.reshape(HEADS, HEAD_SIZE)
    current = guess
    for repeat in range(SWEEPS):
        prior = jnp.concatenate([initial[None, :], current[:-1]], axis=0).reshape(total, HEADS, HEAD_SIZE)
        linear = jnp.einsum("hij,thj->thi", rec_weight, prior, precision=lax.Precision.HIGHEST)
        value = jnp.tanh(linear + drive)
        slope = 1.0 - value * value
        offset = value - slope * linear

        def advance(state, pieces):
            slope_now, offset_now = pieces
            state = slope_now * jnp.einsum("hij,hj->hi", rec_weight, state, precision=lax.Precision.HIGHEST) + offset_now
            return state, state

        ending, states = lax.scan(advance, start_state, (slope, offset))
        current = states.reshape(total, HEADS * HEAD_SIZE)
    tail = jnp.broadcast_to(current[-1][None, :], (SLAB, HEADS * HEAD_SIZE))
    next_guess = jnp.concatenate([current[SLAB:], tail], axis=0)
    return current, next_guess
```

```python
import jax
import jax.numpy as jnp
from jax import lax
from jax.experimental import pallas as pl
from jax.experimental.pallas import tpu as pltpu
from jax.sharding import PartitionSpec as P

MESH = pl.DeviceIdType.MESH
F32 = jnp.float32
BF16 = jnp.bfloat16
U = 128
L = 16
B = 32
GB = 8
NG = B // GB
R = GB * L
T = B * L
PAD = 8
M = U + 16
NX = 4
NY = 4
NZ = 4


def split(value):
    high = value.astype(BF16)
    low = (value - high.astype(F32)).astype(BF16)
    return high, low


def pair(value):
    return jnp.concatenate(split(value), axis=1)


def folded(product):
    return product[:, :U] + product[:, U:]


def twice(block):
    return jnp.concatenate([block, block], axis=0)


def dot(a, b):
    return jnp.dot(a, b, preferred_element_type=F32)


def store_pair(ref, rows, value):
    high, low = split(value)
    ref[rows, 0:U] = high
    ref[rows, U : 2 * U] = low


def combine(first, later, out):
    matrix = later[0:U, :]
    product = folded(dot(first[...], twice(matrix)))
    vector = later[U:M, 0:U].astype(F32) + later[U:M, U : 2 * U].astype(F32)
    store_pair(out, pl.ds(0, U), product[0:U])
    store_pair(out, pl.ds(U, M - U), product[U:M] + vector)


def apply_map(state, ref):
    vector = ref[U:M, 0:U].astype(F32) + ref[U:M, U : 2 * U].astype(F32)
    return folded(dot(pair(state), twice(ref[0:U, :]))) + vector


def kernel(
    x_ref, inw_ref, rec_ref, bias_ref, init_ref, guess_ref,
    traj_ref, next_ref,
    xg, inw, wc, cur, drive, slope, offset, work, leaf, node1, node2, node3, node4, mx, my, half, edge, fill,
    local_sem, xs_sem, xr_sem, mxs_sem, mxr_sem, mys_sem, myr_sem, es_sem, er_sem, ns_sem, nr_sem,
):
    tm = lax.axis_index("tm")
    hd = lax.axis_index("head")
    my_x = lax.rem(tm, NX)
    my_y = tm // NX
    my_z = hd // 2
    core = lax.rem(hd, 2)
    turn = 1 - 2 * core
    partner = my_z * 2 + 1 - core
    ahead_z = lax.rem(my_z + turn + NZ, NZ) * 2 + core
    back_z = lax.rem(my_z - turn + NZ, NZ) * 2 + core
    far_z = lax.rem(my_z + 2, NZ) * 2 + core

    def remote(src, dst, ssem, rsem, to):
        return pltpu.make_async_remote_copy(
            src_ref=src, dst_ref=dst, send_sem=ssem, recv_sem=rsem, device_id=to, device_id_type=MESH
        )

    guess_in = [
        pltpu.make_async_copy(
            guess_ref.at[:, pl.ds(h * U, U)], cur.at[h, pl.ds(PAD, T)], local_sem.at[h]
        )
        for h in range(2)
    ]
    weight_in = pltpu.make_async_copy(inw_ref, inw, local_sem.at[2])
    own_in = pltpu.make_async_copy(x_ref, xg.at[hd], local_sem.at[3])
    own_in.start()
    weight_in.start()
    for copy in guess_in:
        copy.start()

    barrier = pltpu.get_barrier_semaphore()

    def greet(a, b):
        pl.semaphore_signal(barrier, inc=1, device_id=(a, b), device_id_type=MESH)

    greet(tm, partner)
    greet(tm, ahead_z)
    greet(tm, back_z)
    for k in range(1, NX):
        greet(my_y * NX + lax.rem(my_x + k, NX), hd)
    for k in range(1, NY):
        greet(lax.rem(my_y + k, NY) * NX + my_x, hd)
    turns_up = jnp.logical_and(my_x == NX - 1, my_y < NY - 1)
    turns_down = jnp.logical_and(my_x == 0, my_y > 0)

    @pl.when(turns_up)
    def _():
        greet(tm + 1, hd)

    @pl.when(turns_down)
    def _():
        greet(tm - 1, hd)

    turning = jnp.logical_or(turns_up, turns_down).astype(jnp.int32)
    pl.semaphore_wait(barrier, 3 + NX - 1 + NY - 1 + turning)

    def chunk_of(g):
        return pl.ds(pl.multiple_of(g * R, R), R)

    def own_chunk(g, kind, to):
        rows = chunk_of(g)
        return remote(
            x_ref.at[rows], xg.at[hd, rows], xs_sem.at[kind, g], xr_sem.at[hd, g], (tm, to)
        )

    def held_chunk(g, kind, source, to):
        rows = chunk_of(g)
        return remote(
            xg.at[source, rows], xg.at[source, rows], xs_sem.at[kind, g], xr_sem.at[source, g], (tm, to)
        )

    def start_own(g, carry):
        own_chunk(g, 0, ahead_z).start()
        own_chunk(g, 1, back_z).start()
        own_chunk(g, 2, partner).start()
        return carry

    lax.fori_loop(0, NG, start_own, 0)

    edge_copy = remote(
        guess_ref.at[pl.ds(T - 8, 8), :], edge, es_sem.at[0], er_sem.at[0],
        (lax.rem(tm + 1, NX * NY), hd),
    )

    @pl.when(tm < NX * NY - 1)
    def _():
        edge_copy.start()

    for h in range(2):
        transposed = rec_ref[h].T
        high, low = split(transposed)
        for k in range(2):
            wc[h, pl.ds(k * U, U), 0:U] = high
            wc[h, pl.ds(k * U, U), U : 2 * U] = low

    for copy in guess_in:
        copy.wait()

    @pl.when(tm == 0)
    def _():
        for h in range(2):
            cur[h, PAD - 1 : PAD, :] = init_ref[h : h + 1, :]

    @pl.when(tm > 0)
    def _():
        edge_copy.wait_recv()
        for h in range(2):
            cur[h, PAD - 1 : PAD, :] = edge[7:8, h * U : (h + 1) * U]

    own_in.wait()
    weight_in.wait()

    def gather_chunk(g):
        held_chunk(g, 3, back_z, ahead_z).wait_recv()
        held_chunk(g, 3, back_z, ahead_z).start()
        held_chunk(g, 4, back_z, partner).start()
        held_chunk(g, 5, ahead_z, partner).wait_recv()
        held_chunk(g, 5, ahead_z, partner).start()
        held_chunk(g, 6, far_z, partner).wait_recv()
        held_chunk(g, 6, far_z, partner).start()
        for z in range(NZ):
            source = z * 2 + 1 - core
            held_chunk(g, 2, source, partner).wait_recv()
        rows = chunk_of(g)
        total = dot(xg[0, rows, :], inw[0 : 2 * U, :])
        for s in range(1, 2 * NZ):
            total += dot(xg[s, rows, :], inw[s * 2 * U : (s + 1) * 2 * U, :])
        for h in range(2):
            drive[h, rows, :] = total[:, h * U : (h + 1) * U] + bias_ref[h : h + 1, :]

    def compose(h, g):
        base = pl.multiple_of(g * R, R)
        weight = wc[h]
        prior = cur[h, pl.ds(base + (PAD - 1), R), :]
        linear = folded(dot(pair(prior), weight))
        value = jnp.tanh(linear + drive[h, pl.ds(base, R), :])
        steep = 1.0 - value * value
        slope[h, pl.ds(base, R), :] = steep
        offset[h, pl.ds(base, R), :] = value - steep * linear
        transposed = rec_ref[h].T
        for b in range(GB):
            row = slope[h, pl.ds(base + b * L, 1), :]
            store_pair(work.at[b], pl.ds(0, U), transposed * row)
        vector = offset[h, pl.ds(base, GB, stride=L), :]
        for step in range(1, L):
            for b in range(GB):
                row = slope[h, pl.ds(base + b * L + step, 1), :]
                product = folded(dot(work[b], weight)) * row
                out = leaf.at[h, g * GB + b] if step == L - 1 else work.at[b]
                store_pair(out, pl.ds(0, U), product)
            wide = folded(dot(pair(twice(vector)), weight))[0:GB]
            vector = wide * slope[h, pl.ds(base + step, GB, stride=L), :]
            vector = vector + offset[h, pl.ds(base + step, GB, stride=L), :]
        for b in range(GB):
            repeated = jnp.broadcast_to(vector[b : b + 1, :], (M - U, U))
            store_pair(leaf.at[h, g * GB + b], pl.ds(U, M - U), repeated)
        for k in range(4):
            combine(leaf.at[h, g * 8 + 2 * k], leaf.at[h, g * 8 + 2 * k + 1], node1.at[h, g * 4 + k])
        for k in range(2):
            combine(node1.at[h, g * 4 + 2 * k], node1.at[h, g * 4 + 2 * k + 1], node2.at[h, g * 2 + k])
        combine(node2.at[h, g * 2], node2.at[h, g * 2 + 1], node3.at[h, g])

    def row_copy(unit, k):
        return remote(
            mx.at[unit, my_x], mx.at[unit, my_x], mxs_sem.at[unit, k], mxr_sem.at[unit, my_x],
            (my_y * NX + lax.rem(my_x + k, NX), hd),
        )

    def row_arrival(unit, k):
        other = lax.rem(my_x + k, NX)
        return remote(
            mx.at[unit, other], mx.at[unit, other], mxs_sem.at[unit, k], mxr_sem.at[unit, other],
            (my_y * NX + other, hd),
        )

    def column_copy(unit, y):
        return remote(
            my.at[unit, my_y], my.at[unit, my_y], mys_sem.at[unit, y], myr_sem.at[unit, my_y],
            (y * NX + my_x, hd),
        )

    def column_arrival(unit, y):
        return remote(
            my.at[unit, y], my.at[unit, y], mys_sem.at[unit, y], myr_sem.at[unit, y],
            (y * NX + my_x, hd),
        )

    def close_slab(h, unit):
        for k in range(2):
            combine(node3.at[h, 2 * k], node3.at[h, 2 * k + 1], node4.at[h, k])
        combine(node4.at[h, 0], node4.at[h, 1], mx.at[unit, my_x])
        for k in range(1, NX):
            row_copy(unit, k).start()

    def exchange_rows(unit):
        for k in range(1, NX):
            row_arrival(unit, k).wait_recv()
        combine(mx.at[unit, 0], mx.at[unit, 1], half.at[0])
        combine(mx.at[unit, 2], mx.at[unit, 3], half.at[1])
        combine(half.at[0], half.at[1], my.at[unit, my_y])
        for y in range(1, NY):

            @pl.when(my_y < y)
            def _():
                column_copy(unit, y).start()

    def finish(h, unit):
        for y in range(NY - 1):

            @pl.when(my_y > y)
            def _():
                column_arrival(unit, y).wait_recv()

        fill[0:16, :] = jnp.broadcast_to(init_ref[pl.ds(h, 1), :], (16, U))
        for y in range(NY - 1):

            @pl.when(my_y > y)
            def _():
                fill[0:16, :] = apply_map(fill[0:16, :], my.at[unit, y])

        for x in range(NX - 1):

            @pl.when(my_x > x)
            def _():
                fill[0:16, :] = apply_map(fill[0:16, :], mx.at[unit, x])

        entering = fill[0:16, :]
        cur[h, PAD - 1 : PAD, :] = entering[0:1]
        starts = [entering]
        for level, node in ((2, node4), (4, node3), (8, node2), (16, node1), (32, leaf)):
            later = []
            for k in range(level // 2):
                later.append(starts[k])
                later.append(apply_map(starts[k], node.at[h, 2 * k]))
            starts = later
        state = jnp.concatenate([one[0:1] for one in starts], axis=0)
        weight = wc[h]
        for step in range(L):
            linear = folded(dot(pair(state), weight))
            state = linear * slope[h, pl.ds(step, B, stride=L), :]
            state = state + offset[h, pl.ds(step, B, stride=L), :]
            cur[h, pl.ds(PAD + step, B, stride=L), :] = state

    def unit_step(u, carry):
        sweep = u // 8
        h = lax.rem(u // 4, 2)
        g = lax.rem(u, 4)

        @pl.when(u < 4)
        def _():
            gather_chunk(g)

        @pl.when(jnp.logical_and(g == 0, u >= 8))
        def _():
            finish(h, h)

        for unit, place in ((0, 6), (1, 9), (2, 13)):

            @pl.when(u == place)
            def _():
                exchange_rows(unit)

        compose(h, g)

        @pl.when(g == NG - 1)
        def _():
            close_slab(h, sweep * 2 + h)

        return carry

    lax.fori_loop(0, 16, unit_step, 0)

    def out_copy(h):
        return pltpu.make_async_copy(
            cur.at[h, pl.ds(PAD, T)], traj_ref.at[:, pl.ds(h * U, U)], local_sem.at[h]
        )

    def next_copy(h):
        return remote(
            cur.at[h, pl.ds(PAD, T)], next_ref.at[:, pl.ds(h * U, U)], ns_sem.at[h], nr_sem.at[h],
            (lax.rem(tm + NX * NY - 1, NX * NY), hd),
        )

    def fill_copy(h):
        return pltpu.make_async_copy(
            fill.at[pl.ds(0, T)], next_ref.at[:, pl.ds(h * U, U)], local_sem.at[2 + h]
        )

    for h in range(2):
        finish(h, 2 + h)
        out_copy(h).start()

        @pl.when(tm > 0)
        def _():
            next_copy(h).start()

        if h == 0:
            exchange_rows(3)

    @pl.when(tm == NX * NY - 1)
    def _():
        for h in range(2):
            fill[...] = jnp.broadcast_to(cur[h, PAD + T - 1 : PAD + T, :], (T, U))
            fill_copy(h).start()
            fill_copy(h).wait()

    def drain(g, carry):
        for kind, to in ((0, ahead_z), (1, back_z), (2, partner)):
            own_chunk(g, kind, to).wait_send()
        held_chunk(g, 3, back_z, ahead_z).wait_send()
        for kind, source in ((4, back_z), (5, ahead_z), (6, far_z)):
            held_chunk(g, kind, source, partner).wait_send()
        return carry

    lax.fori_loop(0, NG, drain, 0)

    @pl.when(tm < NX * NY - 1)
    def _():
        edge_copy.wait_send()

    for unit in range(4):
        for k in range(1, NX):
            row_copy(unit, k).wait_send()
        for y in range(1, NY):

            @pl.when(my_y < y)
            def _():
                column_copy(unit, y).wait_send()

    for h in range(2):
        out_copy(h).wait()

        @pl.when(tm > 0)
        def _():
            next_copy(h).wait_send()

        @pl.when(tm < NX * NY - 1)
        def _():
            next_copy(h).wait_recv()


def shards(inputs, in_weight, rec_weight, bias, initial, guess):
    vmem = pl.BlockSpec(memory_space=pltpu.VMEM)
    anywhere = pl.BlockSpec(memory_space=pl.ANY)
    out = jax.ShapeDtypeStruct((T, 2 * U), F32)
    dma = pltpu.SemaphoreType.DMA
    return pl.pallas_call(
        kernel,
        out_shape=(out, out),
        in_specs=[anywhere, anywhere, vmem, vmem, vmem, anywhere],
        out_specs=(anywhere, anywhere),
        scratch_shapes=[
            pltpu.VMEM((2 * NZ, T, 2 * U), BF16),
            pltpu.VMEM((2 * NZ * 2 * U, 2 * U), BF16),
            pltpu.VMEM((2, 2 * U, 2 * U), BF16),
            pltpu.VMEM((2, PAD + T, U), F32),
            pltpu.VMEM((2, T, U), F32),
            pltpu.VMEM((2, T, U), F32),
            pltpu.VMEM((2, T, U), F32),
            pltpu.VMEM((GB, U, 2 * U), BF16),
            pltpu.VMEM((2, B, M, 2 * U), BF16),
            pltpu.VMEM((2, 16, M, 2 * U), BF16),
            pltpu.VMEM((2, 8, M, 2 * U), BF16),
            pltpu.VMEM((2, 4, M, 2 * U), BF16),
            pltpu.VMEM((2, 2, M, 2 * U), BF16),
            pltpu.VMEM((4, NX, M, 2 * U), BF16),
            pltpu.VMEM((4, NY, M, 2 * U), BF16),
            pltpu.VMEM((2, M, 2 * U), BF16),
            pltpu.VMEM((8, 2 * U), F32),
            pltpu.VMEM((T, U), F32),
            dma((4,)),
            dma((7, NG)),
            dma((2 * NZ, NG)),
            dma((4, NX)),
            dma((4, NX)),
            dma((4, NY)),
            dma((4, NY)),
            dma((1,)),
            dma((1,)),
            dma((2,)),
            dma((2,)),
        ],
        compiler_params=pltpu.CompilerParams(
            collective_id=0, has_side_effects=True, vmem_limit_bytes=56 * 1024 * 1024
        ),
    )(
        inputs,
        in_weight,
        rec_weight,
        bias.reshape(2, U),
        initial.reshape(2, U),
        guess,
    )


def solution(mesh):
    in_specs = (
        P("tm", "head"),
        P(None, "head"),
        P("head", None, None),
        P("head"),
        P("head"),
        P("tm", "head"),
    )
    out_specs = (P("tm", "head"), P("tm", "head"))
    return jax.shard_map(
        shards, mesh=mesh, in_specs=in_specs, out_specs=out_specs, check_vma=False
    )
```

```python
import jax
import jax.numpy as jnp
from jax import lax
from jax.experimental import pallas as pl
from jax.experimental.pallas import tpu as pltpu
from jax.sharding import PartitionSpec as P

MESH = pl.DeviceIdType.MESH
F32 = jnp.float32
BF16 = jnp.bfloat16
U = 128
NB = 8
NG = 4
L = 16
S = NG * L
R = NB * L
B = NB * NG
T = NB * S
PAD = 8
M = U + 16
NX = 4
NY = 4
NZ = 4


def split(value):
    high = value.astype(BF16)
    low = (value - high.astype(F32)).astype(BF16)
    return high, low


def pair(value):
    return jnp.concatenate(split(value), axis=1)


def folded(product):
    return product[:, :U] + product[:, U:]


def twice(block):
    return jnp.concatenate([block, block], axis=0)


def dot(a, b):
    return jnp.dot(a, b, preferred_element_type=F32)


def store_pair(ref, rows, value):
    high, low = split(value)
    ref[rows, 0:U] = high
    ref[rows, U : 2 * U] = low


def combine(first, later, out):
    matrix = later[0:U, :]
    product = folded(dot(first[...], twice(matrix)))
    vector = later[U:M, 0:U].astype(F32) + later[U:M, U : 2 * U].astype(F32)
    store_pair(out, pl.ds(0, U), product[0:U])
    store_pair(out, pl.ds(U, M - U), product[U:M] + vector)


def apply_map(state, ref):
    vector = ref[U:M, 0:U].astype(F32) + ref[U:M, U : 2 * U].astype(F32)
    return folded(dot(pair(state), twice(ref[0:U, :]))) + vector


def kernel(
    x_ref, inw_ref, rec_hbm, bias_hbm, init_hbm, guess_ref,
    traj_ref, next_ref,
    rec_ref, bias_ref, init_ref, xg, inw, wc, cur, drive, slope, offset, work, leaf, node1, node2, vec, mx, whole, entry, leaving, half, edge, fill,
    local_sem, xs_sem, xr_sem, mxs_sem, mxr_sem, mys_sem, myr_sem, es_sem, er_sem, ns_sem, nr_sem,
):
    tm = lax.axis_index("tm")
    hd = lax.axis_index("head")
    my_x = lax.rem(tm, NX)
    my_y = tm // NX
    my_z = hd // 2
    core = lax.rem(hd, 2)
    turn = 1 - 2 * core
    partner = my_z * 2 + 1 - core
    ahead_z = lax.rem(my_z + turn + NZ, NZ) * 2 + core
    back_z = lax.rem(my_z - turn + NZ, NZ) * 2 + core
    far_z = lax.rem(my_z + 2, NZ) * 2 + core

    def remote(src, dst, ssem, rsem, to):
        return pltpu.make_async_remote_copy(
            src_ref=src, dst_ref=dst, send_sem=ssem, recv_sem=rsem, device_id=to, device_id_type=MESH
        )

    guess_in = [
        pltpu.make_async_copy(
            guess_ref.at[:, pl.ds(h * U, U)], cur.at[h, pl.ds(PAD, T)], local_sem.at[h]
        )
        for h in range(2)
    ]
    weight_in = pltpu.make_async_copy(inw_ref, inw, local_sem.at[2])
    own_in = pltpu.make_async_copy(x_ref, xg.at[hd], local_sem.at[3])
    small_in = [
        pltpu.make_async_copy(src, dst, local_sem.at[4 + k])
        for k, (src, dst) in enumerate(
            ((rec_hbm, rec_ref), (bias_hbm, bias_ref), (init_hbm, init_ref))
        )
    ]
    for copy in small_in:
        copy.start()
    own_in.start()
    weight_in.start()
    for copy in guess_in:
        copy.start()

    barrier = pltpu.get_barrier_semaphore()

    def greet(a, b):
        pl.semaphore_signal(barrier, inc=1, device_id=(a, b), device_id_type=MESH)

    greet(tm, partner)
    greet(tm, ahead_z)
    greet(tm, back_z)
    for k in range(1, NX):
        greet(my_y * NX + lax.rem(my_x + k, NX), hd)
    for k in range(1, NY):
        greet(lax.rem(my_y + k, NY) * NX + my_x, hd)
    turns_up = jnp.logical_and(my_x == NX - 1, my_y < NY - 1)
    turns_down = jnp.logical_and(my_x == 0, my_y > 0)

    @pl.when(turns_up)
    def _():
        greet(tm + 1, hd)

    @pl.when(turns_down)
    def _():
        greet(tm - 1, hd)

    turning = jnp.logical_or(turns_up, turns_down).astype(jnp.int32)
    pl.semaphore_wait(barrier, 3 + NX - 1 + NY - 1 + turning)

    def chunk_of(g):
        return pl.ds(pl.multiple_of(g * L, L), L)

    def own_chunk(g, kind, to):
        rows = chunk_of(g)
        return remote(
            x_ref.at[:, rows], xg.at[hd, :, rows], xs_sem.at[kind, g], xr_sem.at[hd, g], (tm, to)
        )

    def held_chunk(g, kind, source, to):
        rows = chunk_of(g)
        return remote(
            xg.at[source, :, rows], xg.at[source, :, rows], xs_sem.at[kind, g], xr_sem.at[source, g], (tm, to)
        )

    def start_own(g):
        own_chunk(g, 0, ahead_z).start()
        own_chunk(g, 1, back_z).start()
        own_chunk(g, 2, partner).start()

    start_own(0)
    start_own(1)

    edge_copy = remote(
        guess_ref.at[pl.ds(T - 8, 8), :], edge, es_sem.at[0], er_sem.at[0],
        (lax.rem(tm + 1, NX * NY), hd),
    )

    @pl.when(tm < NX * NY - 1)
    def _():
        edge_copy.start()

    for copy in small_in:
        copy.wait()

    for h in range(2):
        transposed = rec_ref[h].T
        high, low = split(transposed)
        for k in range(2):
            wc[h, pl.ds(k * U, U), 0:U] = high
            wc[h, pl.ds(k * U, U), U : 2 * U] = low

    row_id = lax.broadcasted_iota(jnp.int32, (U, U), 0)
    identity = jnp.where(row_id == lax.broadcasted_iota(jnp.int32, (U, U), 1), 1.0, 0.0)
    for h in range(2):
        for b in range(NB):
            store_pair(leaf.at[h, 0, b], pl.ds(0, U), identity)

    for copy in guess_in:
        copy.wait()

    @pl.when(tm == 0)
    def _():
        for h in range(2):
            cur[h, PAD - 1 : PAD, :] = init_ref[h : h + 1, :]

    @pl.when(tm > 0)
    def _():
        edge_copy.wait_recv()
        for h in range(2):
            cur[h, PAD - 1 : PAD, :] = edge[7:8, h * U : (h + 1) * U]

    own_in.wait()
    weight_in.wait()

    def relay_chunk(g):
        held_chunk(g, 3, back_z, ahead_z).wait_recv()
        held_chunk(g, 3, back_z, ahead_z).start()
        held_chunk(g, 4, back_z, partner).start()
        held_chunk(g, 5, ahead_z, partner).wait_recv()
        held_chunk(g, 5, ahead_z, partner).start()

    def far_chunk(g):
        held_chunk(g, 6, far_z, partner).wait_recv()
        held_chunk(g, 6, far_z, partner).start()

    def curve(h, starts, rows, linear):
        through = jnp.concatenate([drive[h, pl.ds(t, rows), :] for t in starts], axis=0)
        value = jnp.tanh(linear + through)
        steep = 1.0 - value * value
        rest = value - steep * linear
        for k, t in enumerate(starts):
            slope[h, pl.ds(t, rows), :] = steep[k * rows : (k + 1) * rows]
            offset[h, pl.ds(t, rows), :] = rest[k * rows : (k + 1) * rows]

    def linear_of(h, starts, rows):
        prior = jnp.concatenate([cur[h, pl.ds(t + (PAD - 1), rows), :] for t in starts], axis=0)
        return folded(dot(pair(prior), wc[h]))

    def gather_chunk(g):
        @pl.when(g == 0)
        def _():
            relay_chunk(0)
            start_own(2)
            far_chunk(0)
            relay_chunk(1)

        @pl.when(g > 0)
        def _():
            far_chunk(g)

        @pl.when(jnp.logical_and(g > 0, g < NG - 1))
        def _():
            relay_chunk(g + 1)

        @pl.when(g == 1)
        def _():
            start_own(3)

        first = pl.multiple_of(g * L, L)
        starts = [first + b * S for b in range(NB)]
        linear = [linear_of(h, starts, L) for h in range(2)]
        for z in range(NZ):
            source = z * 2 + 1 - core
            held_chunk(g, 2, source, partner).wait_recv()
        rows = chunk_of(g)
        total = jnp.zeros((R, 2 * U), F32)
        for s in range(2 * NZ):
            total += dot(xg[s, :, rows, :].reshape(R, 2 * U), inw[s * 2 * U : (s + 1) * 2 * U, :])
        for h in range(2):
            through = total[:, h * U : (h + 1) * U] + bias_ref[h : h + 1, :]
            for k, t in enumerate(starts):
                drive[h, pl.ds(t, L), :] = through[k * L : (k + 1) * L]
            curve(h, starts, L, linear[h])

    def compose(h, g):
        first = pl.multiple_of(g * L, L)
        weight = wc[h]
        vector = jnp.where(g == 0, 0.0, vec[h])
        for step in range(L):
            for b in range(NB):
                row = slope[h, pl.ds(first + (b * S + step), 1), :]
                block = leaf.at[h, g, b] if step == 0 else work.at[b]
                product = folded(dot(block[0:U, :], weight)) * row
                out = leaf.at[h, g + 1, b] if step == L - 1 else work.at[b]
                store_pair(out, pl.ds(0, U), product)
            wide = folded(dot(pair(twice(vector)), weight))[0:NB]
            vector = wide * slope[h, pl.ds(first + step, NB, stride=S), :]
            vector = vector + offset[h, pl.ds(first + step, NB, stride=S), :]
        vec[h] = vector
        for b in range(NB):
            repeated = jnp.broadcast_to(vector[b : b + 1, :], (M - U, U))
            store_pair(leaf.at[h, g + 1, b], pl.ds(U, M - U), repeated)

    def row_copy(unit, k):
        return remote(
            mx.at[unit, my_x], mx.at[unit, my_x], mxs_sem.at[unit, k], mxr_sem.at[unit, my_x],
            (my_y * NX + lax.rem(my_x + k, NX), hd),
        )

    def row_arrival(unit, k):
        other = lax.rem(my_x + k, NX)
        return remote(
            mx.at[unit, other], mx.at[unit, other], mxs_sem.at[unit, k], mxr_sem.at[unit, other],
            (my_y * NX + other, hd),
        )

    def state_copy(unit, y):
        return remote(
            leaving.at[unit], entry.at[unit], mys_sem.at[unit], myr_sem.at[unit],
            (lax.rem(y + 1, NY) * NX + my_x, hd),
        )

    def close_slab(h, unit):
        for k in range(4):
            combine(leaf.at[h, NG, 2 * k], leaf.at[h, NG, 2 * k + 1], node1.at[h, k])
        for k in range(2):
            combine(node1.at[h, 2 * k], node1.at[h, 2 * k + 1], node2.at[h, k])
        combine(node2.at[h, 0], node2.at[h, 1], mx.at[unit, my_x])
        for k in range(1, NX):
            row_copy(unit, k).start()

    def close_row(unit):
        for k in range(1, NX):
            row_arrival(unit, k).wait_recv()
        combine(mx.at[unit, 0], mx.at[unit, 1], half.at[0])
        combine(mx.at[unit, 2], mx.at[unit, 3], half.at[1])
        combine(half.at[0], half.at[1], whole)

    def pass_row(h, unit, y):
        @pl.when(my_y == y)
        def _():
            if y == 0:
                entry[unit] = jnp.broadcast_to(init_ref[h : h + 1, :], (16, U))
            else:
                state_copy(unit, y).wait_recv()
            leaving[unit] = apply_map(entry[unit], whole)
            state_copy(unit, y).start()

    def finish(h, unit):
        @pl.when(my_y == NY - 1)
        def _():
            state_copy(unit, NY - 1).wait_recv()

        fill[0:16, :] = entry[unit]
        for x in range(NX - 1):

            @pl.when(my_x > x)
            def _():
                fill[0:16, :] = apply_map(fill[0:16, :], mx.at[unit, x])

        entering = fill[0:16, :]
        cur[h, PAD - 1 : PAD, :] = entering[0:1]
        starts = [entering]
        for node in (node2.at[h], node1.at[h], leaf.at[h, NG]):
            later = []
            for k in range(len(starts)):
                later.append(starts[k])
                later.append(apply_map(starts[k], node.at[2 * k]))
            starts = later
        states = []
        for b in range(NB):
            states.append(starts[b][0:1])
            for g in range(1, NG):
                states.append(apply_map(starts[b], leaf.at[h, g, b])[0:1])
        state = jnp.concatenate(states, axis=0)
        weight = wc[h]
        for step in range(L):
            linear = folded(dot(pair(state), weight))
            state = linear * slope[h, pl.ds(step, B, stride=L), :]
            state = state + offset[h, pl.ds(step, B, stride=L), :]
            cur[h, pl.ds(PAD + step, B, stride=L), :] = state

    def unit_step(u, carry):
        sweep = u // 8
        h = lax.rem(u // 4, 2)
        g = lax.rem(u, 4)

        @pl.when(u < 4)
        def _():
            gather_chunk(g)

        for unit, closes, passes in ((0, 7, (7, 8, 8)), (1, 9, (9, 10, 11)), (2, 13, (13, 14, 15))):

            @pl.when(u == closes)
            def _():
                close_row(unit)

            for y in range(NY - 1):

                @pl.when(u == passes[y])
                def _():
                    pass_row(unit % 2, unit, y)

        @pl.when(jnp.logical_and(g == 0, u >= 8))
        def _():
            finish(h, h)
            curve(h, [0], T, linear_of(h, [0], T))

        compose(h, g)

        @pl.when(g == NG - 1)
        def _():
            close_slab(h, sweep * 2 + h)

        return carry

    lax.fori_loop(0, 16, unit_step, 0)

    def out_copy(h):
        return pltpu.make_async_copy(
            cur.at[h, pl.ds(PAD, T)], traj_ref.at[:, pl.ds(h * U, U)], local_sem.at[h]
        )

    def next_copy(h):
        return remote(
            cur.at[h, pl.ds(PAD, T)], next_ref.at[:, pl.ds(h * U, U)], ns_sem.at[h], nr_sem.at[h],
            (lax.rem(tm + NX * NY - 1, NX * NY), hd),
        )

    def fill_copy(h):
        return pltpu.make_async_copy(
            fill.at[pl.ds(0, T)], next_ref.at[:, pl.ds(h * U, U)], local_sem.at[2 + h]
        )

    for h in range(2):
        finish(h, 2 + h)
        out_copy(h).start()

        @pl.when(tm > 0)
        def _():
            next_copy(h).start()

        if h == 0:
            close_row(3)
            for y in range(NY - 1):
                pass_row(1, 3, y)

    @pl.when(tm == NX * NY - 1)
    def _():
        for h in range(2):
            fill[...] = jnp.broadcast_to(cur[h, PAD + T - 1 : PAD + T, :], (T, U))
            fill_copy(h).start()
            fill_copy(h).wait()

    def drain(g, carry):
        for kind, to in ((0, ahead_z), (1, back_z), (2, partner)):
            own_chunk(g, kind, to).wait_send()
        held_chunk(g, 3, back_z, ahead_z).wait_send()
        for kind, source in ((4, back_z), (5, ahead_z), (6, far_z)):
            held_chunk(g, kind, source, partner).wait_send()
        return carry

    lax.fori_loop(0, NG, drain, 0)

    @pl.when(tm < NX * NY - 1)
    def _():
        edge_copy.wait_send()

    for unit in range(4):
        for k in range(1, NX):
            row_copy(unit, k).wait_send()

        @pl.when(my_y < NY - 1)
        def _():
            state_copy(unit, my_y).wait_send()

    for h in range(2):
        out_copy(h).wait()

        @pl.when(tm > 0)
        def _():
            next_copy(h).wait_send()

        @pl.when(tm < NX * NY - 1)
        def _():
            next_copy(h).wait_recv()


def shards(inputs, in_weight, rec_weight, bias, initial, guess):
    hbm = pl.BlockSpec(memory_space=pltpu.HBM)
    anywhere = pl.BlockSpec(memory_space=pl.ANY)
    out = jax.ShapeDtypeStruct((T, 2 * U), F32)
    dma = pltpu.SemaphoreType.DMA
    return pl.pallas_call(
        kernel,
        out_shape=(out, out),
        in_specs=[hbm] * 6,
        out_specs=(anywhere, anywhere),
        scratch_shapes=[
            pltpu.VMEM((2, U, U), F32),
            pltpu.VMEM((2, U), F32),
            pltpu.VMEM((2, U), F32),
            pltpu.VMEM((2 * NZ, NB, S, 2 * U), BF16),
            pltpu.VMEM((2 * NZ * 2 * U, 2 * U), BF16),
            pltpu.VMEM((2, 2 * U, 2 * U), BF16),
            pltpu.VMEM((2, PAD + T, U), F32),
            pltpu.VMEM((2, T, U), F32),
            pltpu.VMEM((2, T, U), F32),
            pltpu.VMEM((2, T, U), F32),
            pltpu.VMEM((NB, U, 2 * U), BF16),
            pltpu.VMEM((2, NG + 1, NB, M, 2 * U), BF16),
            pltpu.VMEM((2, 4, M, 2 * U), BF16),
            pltpu.VMEM((2, 2, M, 2 * U), BF16),
            pltpu.VMEM((2, NB, U), F32),
            pltpu.VMEM((4, NX, M, 2 * U), BF16),
            pltpu.VMEM((M, 2 * U), BF16),
            pltpu.VMEM((4, 16, U), F32),
            pltpu.VMEM((4, 16, U), F32),
            pltpu.VMEM((2, M, 2 * U), BF16),
            pltpu.VMEM((8, 2 * U), F32),
            pltpu.VMEM((T, U), F32),
            dma((7,)),
            dma((7, NG)),
            dma((2 * NZ, NG)),
            dma((4, NX)),
            dma((4, NX)),
            dma((4,)),
            dma((4,)),
            dma((1,)),
            dma((1,)),
            dma((2,)),
            dma((2,)),
        ],
        compiler_params=pltpu.CompilerParams(
            collective_id=0, has_side_effects=True, vmem_limit_bytes=56 * 1024 * 1024
        ),
    )(
        inputs.reshape(NB, S, 2 * U),
        in_weight,
        rec_weight,
        bias.reshape(2, U),
        initial.reshape(2, U),
        guess,
    )


def solution(mesh):
    in_specs = (
        P("tm", "head"),
        P(None, "head"),
        P("head", None, None),
        P("head"),
        P("head"),
        P("tm", "head"),
    )
    out_specs = (P("tm", "head"), P("tm", "head"))
    return jax.shard_map(
        shards, mesh=mesh, in_specs=in_specs, out_specs=out_specs, check_vma=False
    )
```

```python
import jax
import jax.numpy as jnp
from jax import lax
from jax.experimental import pallas as pl
from jax.experimental.pallas import tpu as pltpu
from jax.sharding import PartitionSpec as P

MESH = pl.DeviceIdType.MESH
F32 = jnp.float32
BF16 = jnp.bfloat16
U = 128
NB = 8
NG = 4
L = 16
S = NG * L
R = NB * L
B = NB * NG
T = NB * S
PAD = 8
M = U + 16
NX = 4
NY = 4
NZ = 4


def split(value):
    high = value.astype(BF16)
    low = (value - high.astype(F32)).astype(BF16)
    return high, low


def pair(value):
    return jnp.concatenate(split(value), axis=1)


def folded(product):
    return product[:, :U] + product[:, U:]


def twice(block):
    return jnp.concatenate([block, block], axis=0)


def dot(a, b):
    return jnp.dot(a, b, preferred_element_type=F32)


def store_pair(ref, rows, value):
    high, low = split(value)
    ref[rows, 0:U] = high
    ref[rows, U : 2 * U] = low


def combine(first, later, out):
    matrix = later[0:U, :]
    product = folded(dot(first[...], twice(matrix)))
    vector = later[U:M, 0:U].astype(F32) + later[U:M, U : 2 * U].astype(F32)
    store_pair(out, pl.ds(0, U), product[0:U])
    store_pair(out, pl.ds(U, M - U), product[U:M] + vector)


def apply_map(state, ref):
    vector = ref[U:M, 0:U].astype(F32) + ref[U:M, U : 2 * U].astype(F32)
    return folded(dot(pair(state), twice(ref[0:U, :]))) + vector


def kernel(
    x_ref, inw_ref, rec_hbm, bias_hbm, init_hbm, guess_ref,
    traj_ref, next_ref,
    rec_ref, bias_ref, init_ref, xg, inw, wc, cur, drive, slope, offset, work, leaf, node1, node2, vec, mx, whole, entry, leaving, half, edge, fill,
    ndrive, ncur, nslope, noffset, origin, norigin, ahead,
    local_sem, xs_sem, xr_sem, mxs_sem, mxr_sem, mys_sem, myr_sem, es_sem, er_sem, ns_sem, nr_sem,
    nds_sem, ndr_sem, ncs_sem, ncr_sem,
):
    tm = lax.axis_index("tm")
    hd = lax.axis_index("head")
    my_x = lax.rem(tm, NX)
    my_y = tm // NX
    my_z = hd // 2
    core = lax.rem(hd, 2)
    turn = 1 - 2 * core
    partner = my_z * 2 + 1 - core
    ahead_z = lax.rem(my_z + turn + NZ, NZ) * 2 + core
    back_z = lax.rem(my_z - turn + NZ, NZ) * 2 + core
    far_z = lax.rem(my_z + 2, NZ) * 2 + core
    across = ahead_z + turn

    def remote(src, dst, ssem, rsem, to):
        return pltpu.make_async_remote_copy(
            src_ref=src, dst_ref=dst, send_sem=ssem, recv_sem=rsem, device_id=to, device_id_type=MESH
        )

    guess_in = [
        pltpu.make_async_copy(
            guess_ref.at[:, pl.ds(h * U, U)], cur.at[h, pl.ds(PAD, T)], local_sem.at[h]
        )
        for h in range(2)
    ]
    weight_in = pltpu.make_async_copy(inw_ref, inw, local_sem.at[2])
    own_in = pltpu.make_async_copy(x_ref, xg.at[hd], local_sem.at[3])
    small_in = [
        pltpu.make_async_copy(src, dst, local_sem.at[4 + k])
        for k, (src, dst) in enumerate(
            ((rec_hbm, rec_ref), (bias_hbm, bias_ref), (init_hbm, init_ref))
        )
    ]
    for copy in small_in:
        copy.start()
    own_in.start()
    weight_in.start()
    for copy in guess_in:
        copy.start()

    barrier = pltpu.get_barrier_semaphore()

    def greet(a, b):
        pl.semaphore_signal(barrier, inc=1, device_id=(a, b), device_id_type=MESH)

    greet(tm, partner)
    greet(tm, ahead_z)
    greet(tm, back_z)
    greet(tm, across)
    for k in range(1, NX):
        greet(my_y * NX + lax.rem(my_x + k, NX), hd)
    for k in range(1, NY):
        greet(lax.rem(my_y + k, NY) * NX + my_x, hd)
    turns_up = jnp.logical_and(my_x == NX - 1, my_y < NY - 1)
    turns_down = jnp.logical_and(my_x == 0, my_y > 0)

    @pl.when(turns_up)
    def _():
        greet(tm + 1, hd)

    @pl.when(turns_down)
    def _():
        greet(tm - 1, hd)

    turning = jnp.logical_or(turns_up, turns_down).astype(jnp.int32)
    pl.semaphore_wait(barrier, 4 + NX - 1 + NY - 1 + turning)

    def chunk_of(g):
        return pl.ds(pl.multiple_of(g * L, L), L)

    def own_chunk(g, kind, to):
        rows = chunk_of(g)
        return remote(
            x_ref.at[:, rows], xg.at[hd, :, rows], xs_sem.at[kind, g], xr_sem.at[hd, g], (tm, to)
        )

    def held_chunk(g, kind, source, to):
        rows = chunk_of(g)
        return remote(
            xg.at[source, :, rows], xg.at[source, :, rows], xs_sem.at[kind, g], xr_sem.at[source, g], (tm, to)
        )

    def start_own(g):
        own_chunk(g, 0, ahead_z).start()
        own_chunk(g, 1, back_z).start()
        own_chunk(g, 2, partner).start()

    start_own(0)
    start_own(1)

    edge_copy = remote(
        guess_ref.at[pl.ds(T - 8, 8), :], edge, es_sem.at[0], er_sem.at[0],
        (lax.rem(tm + 1, NX * NY), hd),
    )

    @pl.when(tm < NX * NY - 1)
    def _():
        edge_copy.start()

    for copy in small_in:
        copy.wait()

    for h in range(2):
        transposed = rec_ref[h].T
        high, low = split(transposed)
        for k in range(2):
            wc[h, pl.ds(k * U, U), 0:U] = high
            wc[h, pl.ds(k * U, U), U : 2 * U] = low

    row_id = lax.broadcasted_iota(jnp.int32, (U, U), 0)
    identity = jnp.where(row_id == lax.broadcasted_iota(jnp.int32, (U, U), 1), 1.0, 0.0)
    for h in range(2):
        for b in range(NB):
            store_pair(leaf.at[h, 0, b], pl.ds(0, U), identity)

    for copy in guess_in:
        copy.wait()

    @pl.when(tm == 0)
    def _():
        for h in range(2):
            cur[h, PAD - 1 : PAD, :] = init_ref[h : h + 1, :]

    @pl.when(tm > 0)
    def _():
        edge_copy.wait_recv()
        for h in range(2):
            cur[h, PAD - 1 : PAD, :] = edge[7:8, h * U : (h + 1) * U]

    own_in.wait()
    weight_in.wait()

    def relay_chunk(g):
        held_chunk(g, 3, back_z, ahead_z).wait_recv()
        held_chunk(g, 3, back_z, ahead_z).start()
        held_chunk(g, 6, back_z, across).start()
        held_chunk(g, 4, back_z, partner).start()
        held_chunk(g, 5, ahead_z, partner).wait_recv()
        held_chunk(g, 5, ahead_z, partner).start()

    def curve(h, starts, rows, linear, through, slope=slope, offset=offset):
        value = jnp.tanh(linear + through)
        steep = 1.0 - value * value
        rest = value - steep * linear
        for k, t in enumerate(starts):
            slope[h, pl.ds(t, rows), :] = steep[k * rows : (k + 1) * rows]
            offset[h, pl.ds(t, rows), :] = rest[k * rows : (k + 1) * rows]

    def linear_of(h, starts, rows, cur=cur):
        prior = jnp.concatenate([cur[h, pl.ds(t + (PAD - 1), rows), :] for t in starts], axis=0)
        return folded(dot(pair(prior), wc[h]))

    previous = (lax.rem(tm + NX * NY - 1, NX * NY), hd)

    def drive_copy(g):
        rows = chunk_of(g)
        return remote(
            drive.at[:, :, rows], ndrive.at[:, :, rows], nds_sem.at[g], ndr_sem.at[g], previous
        )

    def path_copy(h):
        steps = pl.ds(PAD, T)
        return remote(cur.at[h, steps], ncur.at[h, steps], ncs_sem.at[h], ncr_sem.at[h], previous)

    def start_copy(h):
        return remote(origin.at[h], norigin.at[h], ns_sem.at[h], nr_sem.at[h], previous)

    def gather_chunk(g):
        @pl.when(g == 0)
        def _():
            relay_chunk(0)
            start_own(2)
            relay_chunk(1)

        @pl.when(jnp.logical_and(g > 0, g < NG - 1))
        def _():
            relay_chunk(g + 1)

        @pl.when(g == 1)
        def _():
            start_own(3)

        first = pl.multiple_of(g * L, L)
        starts = [first + b * S for b in range(NB)]
        linear = [linear_of(h, starts, L) for h in range(2)]
        held_chunk(g, 3, far_z, ahead_z).wait_recv()
        for z in range(NZ):
            source = z * 2 + 1 - core
            held_chunk(g, 2, source, partner).wait_recv()
        rows = chunk_of(g)
        total = jnp.zeros((R, 2 * U), F32)
        for s in range(2 * NZ):
            total += dot(xg[s, :, rows, :].reshape(R, 2 * U), inw[s * 2 * U : (s + 1) * 2 * U, :])
        for h in range(2):
            through = total[:, h * U : (h + 1) * U] + bias_ref[h : h + 1, :]
            drive[h, :, rows, :] = through.reshape(NB, L, U)
            curve(h, starts, L, linear[h], through)

        @pl.when(tm > 0)
        def _():
            drive_copy(g).start()

    def compose(h, g):
        first = pl.multiple_of(g * L, L)
        weight = wc[h]
        vector = jnp.where(g == 0, 0.0, vec[h])
        for step in range(L):
            for b in range(NB):
                row = slope[h, pl.ds(first + (b * S + step), 1), :]
                block = leaf.at[h, g, b] if step == 0 else work.at[b]
                product = folded(dot(block[0:U, :], weight)) * row
                out = leaf.at[h, g + 1, b] if step == L - 1 else work.at[b]
                store_pair(out, pl.ds(0, U), product)
            wide = folded(dot(pair(twice(vector)), weight))[0:NB]
            vector = wide * slope[h, pl.ds(first + step, NB, stride=S), :]
            vector = vector + offset[h, pl.ds(first + step, NB, stride=S), :]
        vec[h] = vector
        for b in range(NB):
            repeated = jnp.broadcast_to(vector[b : b + 1, :], (M - U, U))
            store_pair(leaf.at[h, g + 1, b], pl.ds(U, M - U), repeated)

    def row_copy(unit, k):
        return remote(
            mx.at[unit, my_x], mx.at[unit, my_x], mxs_sem.at[unit, k], mxr_sem.at[unit, my_x],
            (my_y * NX + lax.rem(my_x + k, NX), hd),
        )

    def row_arrival(unit, k):
        other = lax.rem(my_x + k, NX)
        return remote(
            mx.at[unit, other], mx.at[unit, other], mxs_sem.at[unit, k], mxr_sem.at[unit, other],
            (my_y * NX + other, hd),
        )

    def state_copy(unit, y):
        return remote(
            leaving.at[unit], entry.at[unit], mys_sem.at[unit], myr_sem.at[unit],
            (lax.rem(y + 1, NY) * NX + my_x, hd),
        )

    def close_slab(h, unit):
        for k in range(4):
            combine(leaf.at[h, NG, 2 * k], leaf.at[h, NG, 2 * k + 1], node1.at[h, k])
        for k in range(2):
            combine(node1.at[h, 2 * k], node1.at[h, 2 * k + 1], node2.at[h, k])
        combine(node2.at[h, 0], node2.at[h, 1], mx.at[unit, my_x])
        for k in range(1, NX):
            row_copy(unit, k).start()

    def close_row(unit):
        for k in range(1, NX):
            row_arrival(unit, k).wait_recv()
        combine(mx.at[unit, 0], mx.at[unit, 1], half.at[0])
        combine(mx.at[unit, 2], mx.at[unit, 3], half.at[1])
        combine(half.at[0], half.at[1], whole)

    def pass_row(h, unit, y):
        @pl.when(my_y == y)
        def _():
            if y == 0:
                entry[unit] = jnp.broadcast_to(init_ref[h : h + 1, :], (16, U))
            else:
                state_copy(unit, y).wait_recv()
            leaving[unit] = apply_map(entry[unit], whole)
            state_copy(unit, y).start()

    def finish(h, unit, last=False):
        @pl.when(my_y == NY - 1)
        def _():
            state_copy(unit, NY - 1).wait_recv()

        fill[0:16, :] = entry[unit]
        for x in range(NX - 1):

            @pl.when(my_x > x)
            def _():
                fill[0:16, :] = apply_map(fill[0:16, :], mx.at[unit, x])

        entering = fill[0:16, :]
        cur[h, PAD - 1 : PAD, :] = entering[0:1]
        starts = [entering]
        for node in (node2.at[h], node1.at[h], leaf.at[h, NG]):
            later = []
            for k in range(len(starts)):
                later.append(starts[k])
                later.append(apply_map(starts[k], node.at[2 * k]))
            starts = later
        states = []
        for b in range(NB):
            states.append(starts[b][0:1])
            for g in range(1, NG):
                states.append(apply_map(starts[b], leaf.at[h, g, b])[0:1])
        state = jnp.concatenate(states, axis=0)
        if last:
            origin[h] = state

            @pl.when(tm > 0)
            def _():
                start_copy(h).start()
                path_copy(h).wait_send()

        advance(h, state, slope, offset, cur, PAD)

    def advance(h, state, slope, offset, out, base):
        weight = wc[h]
        for step in range(L):
            linear = folded(dot(pair(state), weight))
            state = linear * slope[h, pl.ds(step, B, stride=L), :]
            state = state + offset[h, pl.ds(step, B, stride=L), :]
            out[h, pl.ds(base + step, B, stride=L), :] = state

    def unit_step(u, carry):
        sweep = u // 8
        h = lax.rem(u // 4, 2)
        g = lax.rem(u, 4)

        @pl.when(u < 4)
        def _():
            gather_chunk(g)

        for unit, closes, passes in ((0, 7, (7, 8, 8)), (1, 9, (9, 10, 11)), (2, 13, (13, 14, 15))):

            @pl.when(u == closes)
            def _():
                close_row(unit)

            for y in range(NY - 1):

                @pl.when(u == passes[y])
                def _():
                    pass_row(unit % 2, unit, y)

        @pl.when(jnp.logical_and(g == 0, u >= 8))
        def _():
            finish(h, h)

            @pl.when(tm > 0)
            def _():
                path_copy(h).start()

            ncur[h, PAD - 1 : PAD, :] = cur[h, PAD + T - 1 : PAD + T, :]
            curve(h, [0], T, linear_of(h, [0], T), drive[h].reshape(T, U))

        compose(h, g)

        @pl.when(g == NG - 1)
        def _():
            close_slab(h, sweep * 2 + h)

        return carry

    lax.fori_loop(0, 16, unit_step, 0)

    def out_copy(h):
        return pltpu.make_async_copy(
            cur.at[h, pl.ds(PAD, T)], traj_ref.at[:, pl.ds(h * U, U)], local_sem.at[h]
        )

    def next_copy(h):
        return pltpu.make_async_copy(
            ahead.at[h], next_ref.at[:, pl.ds(h * U, U)], local_sem.at[2 + h]
        )

    def follow(h):
        @pl.when(tm < NX * NY - 1)
        def _():
            start_copy(h).wait_recv()
            advance(h, norigin[h], nslope, noffset, ahead, 0)

        @pl.when(tm == NX * NY - 1)
        def _():
            ahead[h] = jnp.broadcast_to(cur[h, PAD + T - 1 : PAD + T, :], (T, U))

        next_copy(h).start()

    finish(0, 2, last=True)
    out_copy(0).start()

    def following_curve():
        @pl.when(tm < NX * NY - 1)
        def _():
            for g in range(NG):
                drive_copy(g).wait_recv()
            for h in range(2):
                path_copy(h).wait_recv()
                linear = linear_of(h, [0], T, ncur)
                curve(h, [0], T, linear, ndrive[h].reshape(T, U), nslope, noffset)

    close_row(3)

    @pl.when(my_y > 0)
    def _():
        following_curve()

    @pl.when(my_y >= 2)
    def _():
        follow(0)

    for y in range(NY - 1):
        pass_row(1, 3, y)

    @pl.when(my_y == 0)
    def _():
        following_curve()

    @pl.when(my_y < 2)
    def _():
        follow(0)

    finish(1, 3, last=True)
    out_copy(1).start()
    follow(1)

    def drain(g, carry):
        for kind, to in ((0, ahead_z), (1, back_z), (2, partner)):
            own_chunk(g, kind, to).wait_send()
        held_chunk(g, 3, back_z, ahead_z).wait_send()
        held_chunk(g, 6, back_z, across).wait_send()
        for kind, source in ((4, back_z), (5, ahead_z)):
            held_chunk(g, kind, source, partner).wait_send()
        return carry

    lax.fori_loop(0, NG, drain, 0)

    @pl.when(tm < NX * NY - 1)
    def _():
        edge_copy.wait_send()

    for unit in range(4):
        for k in range(1, NX):
            row_copy(unit, k).wait_send()

        @pl.when(my_y < NY - 1)
        def _():
            state_copy(unit, my_y).wait_send()

    @pl.when(tm > 0)
    def _():
        for g in range(NG):
            drive_copy(g).wait_send()
        for h in range(2):
            start_copy(h).wait_send()

    for h in range(2):
        out_copy(h).wait()
        next_copy(h).wait()


def shards(inputs, in_weight, rec_weight, bias, initial, guess):
    hbm = pl.BlockSpec(memory_space=pltpu.HBM)
    anywhere = pl.BlockSpec(memory_space=pl.ANY)
    out = jax.ShapeDtypeStruct((T, 2 * U), F32)
    dma = pltpu.SemaphoreType.DMA
    return pl.pallas_call(
        kernel,
        out_shape=(out, out),
        in_specs=[hbm] * 6,
        out_specs=(anywhere, anywhere),
        scratch_shapes=[
            pltpu.VMEM((2, U, U), F32),
            pltpu.VMEM((2, U), F32),
            pltpu.VMEM((2, U), F32),
            pltpu.VMEM((2 * NZ, NB, S, 2 * U), BF16),
            pltpu.VMEM((2 * NZ * 2 * U, 2 * U), BF16),
            pltpu.VMEM((2, 2 * U, 2 * U), BF16),
            pltpu.VMEM((2, PAD + T, U), F32),
            pltpu.VMEM((2, NB, S, U), F32),
            pltpu.VMEM((2, T, U), F32),
            pltpu.VMEM((2, T, U), F32),
            pltpu.VMEM((NB, U, 2 * U), BF16),
            pltpu.VMEM((2, NG + 1, NB, M, 2 * U), BF16),
            pltpu.VMEM((2, 4, M, 2 * U), BF16),
            pltpu.VMEM((2, 2, M, 2 * U), BF16),
            pltpu.VMEM((2, NB, U), F32),
            pltpu.VMEM((4, NX, M, 2 * U), BF16),
            pltpu.VMEM((M, 2 * U), BF16),
            pltpu.VMEM((4, 16, U), F32),
            pltpu.VMEM((4, 16, U), F32),
            pltpu.VMEM((2, M, 2 * U), BF16),
            pltpu.VMEM((8, 2 * U), F32),
            pltpu.VMEM((16, U), F32),
            pltpu.VMEM((2, NB, S, U), F32),
            pltpu.VMEM((2, PAD + T, U), F32),
            pltpu.VMEM((2, T, U), F32),
            pltpu.VMEM((2, T, U), F32),
            pltpu.VMEM((2, B, U), F32),
            pltpu.VMEM((2, B, U), F32),
            pltpu.VMEM((2, T, U), F32),
            dma((7,)),
            dma((7, NG)),
            dma((2 * NZ, NG)),
            dma((4, NX)),
            dma((4, NX)),
            dma((4,)),
            dma((4,)),
            dma((1,)),
            dma((1,)),
            dma((2,)),
            dma((2,)),
            dma((NG,)),
            dma((NG,)),
            dma((2,)),
            dma((2,)),
        ],
        compiler_params=pltpu.CompilerParams(
            collective_id=0, has_side_effects=True, vmem_limit_bytes=56 * 1024 * 1024
        ),
    )(
        inputs.reshape(NB, S, 2 * U),
        in_weight,
        rec_weight,
        bias.reshape(2, U),
        initial.reshape(2, U),
        guess,
    )


def solution(mesh):
    in_specs = (
        P("tm", "head"),
        P(None, "head"),
        P("head", None, None),
        P("head"),
        P("head"),
        P("tm", "head"),
    )
    out_specs = (P("tm", "head"), P("tm", "head"))
    return jax.shard_map(
        shards, mesh=mesh, in_specs=in_specs, out_specs=out_specs, check_vma=False
    )
```

```python
import jax
import jax.numpy as jnp
from jax import lax
from jax.experimental import pallas as pl
from jax.experimental.pallas import tpu as pltpu
from jax.sharding import PartitionSpec as P

MESH = pl.DeviceIdType.MESH
F32 = jnp.float32
BF16 = jnp.bfloat16
U = 128
NB = 8
NG = 4
L = 16
S = NG * L
R = NB * L
B = NB * NG
T = NB * S
PAD = 8
M = U + 16
NX = 4
NY = 4
NZ = 4


def split(value):
    high = value.astype(BF16)
    low = (value - high.astype(F32)).astype(BF16)
    return high, low


def pair(value):
    return jnp.concatenate(split(value), axis=1)


def folded(product):
    return product[:, :U] + product[:, U:]


def twice(block):
    return jnp.concatenate([block, block], axis=0)


def dot(a, b):
    return jnp.dot(a, b, preferred_element_type=F32)


def store_pair(ref, rows, value):
    high, low = split(value)
    ref[rows, 0:U] = high
    ref[rows, U : 2 * U] = low


def combine(first, later, out):
    matrix = later[0:U, :]
    product = folded(dot(first[...], twice(matrix)))
    vector = later[U:M, 0:U].astype(F32) + later[U:M, U : 2 * U].astype(F32)
    store_pair(out, pl.ds(0, U), product[0:U])
    store_pair(out, pl.ds(U, M - U), product[U:M] + vector)


def apply_map(state, ref):
    vector = ref[U:M, 0:U].astype(F32) + ref[U:M, U : 2 * U].astype(F32)
    return folded(dot(pair(state), twice(ref[0:U, :]))) + vector


def kernel(
    x_ref, inw_ref, rec_hbm, bias_hbm, init_hbm, guess_ref,
    traj_ref, next_ref,
    rec_ref, bias_ref, init_ref, xg, inw, wc, cur, drive, slope, offset, work, leaf, node1, node2, vec, mx, whole, entry, leaving, half, edge, fill,
    ndrive, ncur, nslope, noffset, origin, norigin, ahead,
    local_sem, xs_sem, xr_sem, mxs_sem, mxr_sem, mys_sem, myr_sem, es_sem, er_sem, ns_sem, nr_sem,
    nds_sem, ndr_sem, ncs_sem, ncr_sem,
):
    tm = lax.axis_index("tm")
    hd = lax.axis_index("head")
    my_x = lax.rem(tm, NX)
    my_y = tm // NX
    my_z = hd // 2
    core = lax.rem(hd, 2)
    turn = 1 - 2 * core
    partner = my_z * 2 + 1 - core
    ahead_z = lax.rem(my_z + turn + NZ, NZ) * 2 + core
    back_z = lax.rem(my_z - turn + NZ, NZ) * 2 + core
    far_z = lax.rem(my_z + 2, NZ) * 2 + core
    across = ahead_z + turn

    def remote(src, dst, ssem, rsem, to):
        return pltpu.make_async_remote_copy(
            src_ref=src, dst_ref=dst, send_sem=ssem, recv_sem=rsem, device_id=to, device_id_type=MESH
        )

    guess_in = [
        pltpu.make_async_copy(
            guess_ref.at[:, pl.ds(h * U, U)], cur.at[h, pl.ds(PAD, T)], local_sem.at[h]
        )
        for h in range(2)
    ]
    weight_in = pltpu.make_async_copy(inw_ref, inw, local_sem.at[2])
    own_in = pltpu.make_async_copy(x_ref, xg.at[hd], local_sem.at[3])
    small_in = [
        pltpu.make_async_copy(src, dst, local_sem.at[4 + k])
        for k, (src, dst) in enumerate(
            ((rec_hbm, rec_ref), (bias_hbm, bias_ref), (init_hbm, init_ref))
        )
    ]
    for copy in small_in:
        copy.start()
    own_in.start()
    weight_in.start()
    for copy in guess_in:
        copy.start()

    barrier = pltpu.get_barrier_semaphore()

    def greet(a, b):
        pl.semaphore_signal(barrier, inc=1, device_id=(a, b), device_id_type=MESH)

    greet(tm, partner)
    greet(tm, ahead_z)
    greet(tm, back_z)
    greet(tm, across)
    for k in range(1, NX):
        greet(my_y * NX + lax.rem(my_x + k, NX), hd)
    for k in range(1, NY):
        greet(lax.rem(my_y + k, NY) * NX + my_x, hd)
    turns_up = jnp.logical_and(my_x == NX - 1, my_y < NY - 1)
    turns_down = jnp.logical_and(my_x == 0, my_y > 0)

    @pl.when(turns_up)
    def _():
        greet(tm + 1, hd)

    @pl.when(turns_down)
    def _():
        greet(tm - 1, hd)

    turning = jnp.logical_or(turns_up, turns_down).astype(jnp.int32)
    pl.semaphore_wait(barrier, 4 + NX - 1 + NY - 1 + turning)

    def chunk_of(g):
        return pl.ds(pl.multiple_of(g * L, L), L)

    def own_chunk(g, kind, to):
        rows = chunk_of(g)
        return remote(
            x_ref.at[:, rows], xg.at[hd, :, rows], xs_sem.at[kind, g], xr_sem.at[hd, g], (tm, to)
        )

    def held_chunk(g, kind, source, to):
        rows = chunk_of(g)
        return remote(
            xg.at[source, :, rows], xg.at[source, :, rows], xs_sem.at[kind, g], xr_sem.at[source, g], (tm, to)
        )

    def start_own(g):
        own_chunk(g, 0, ahead_z).start()
        own_chunk(g, 1, back_z).start()
        own_chunk(g, 2, partner).start()

    start_own(0)
    start_own(1)

    edge_copy = remote(
        guess_ref.at[pl.ds(T - 8, 8), :], edge, es_sem.at[0], er_sem.at[0],
        (lax.rem(tm + 1, NX * NY), hd),
    )

    @pl.when(tm < NX * NY - 1)
    def _():
        edge_copy.start()

    for copy in small_in:
        copy.wait()

    for h in range(2):
        transposed = rec_ref[h].T
        high, low = split(transposed)
        for k in range(2):
            wc[h, pl.ds(k * U, U), 0:U] = high
            wc[h, pl.ds(k * U, U), U : 2 * U] = low

    row_id = lax.broadcasted_iota(jnp.int32, (U, U), 0)
    identity = jnp.where(row_id == lax.broadcasted_iota(jnp.int32, (U, U), 1), 1.0, 0.0)
    for h in range(2):
        for b in range(NB):
            store_pair(leaf.at[h, 0, b], pl.ds(0, U), identity)

    for copy in guess_in:
        copy.wait()

    @pl.when(tm == 0)
    def _():
        for h in range(2):
            cur[h, PAD - 1 : PAD, :] = init_ref[h : h + 1, :]

    @pl.when(tm > 0)
    def _():
        edge_copy.wait_recv()
        for h in range(2):
            cur[h, PAD - 1 : PAD, :] = edge[7:8, h * U : (h + 1) * U]

    own_in.wait()
    weight_in.wait()

    def relay_chunk(g):
        held_chunk(g, 3, back_z, ahead_z).wait_recv()
        held_chunk(g, 3, back_z, ahead_z).start()
        held_chunk(g, 6, back_z, across).start()
        held_chunk(g, 4, back_z, partner).start()
        held_chunk(g, 5, ahead_z, partner).wait_recv()
        held_chunk(g, 5, ahead_z, partner).start()

    def curve(h, starts, rows, linear, through, slope=slope, offset=offset):
        value = jnp.tanh(linear + through)
        steep = 1.0 - value * value
        rest = value - steep * linear
        for k, t in enumerate(starts):
            slope[h, pl.ds(t, rows), :] = steep[k * rows : (k + 1) * rows]
            offset[h, pl.ds(t, rows), :] = rest[k * rows : (k + 1) * rows]

    def linear_of(h, starts, rows, cur=cur):
        prior = jnp.concatenate([cur[h, pl.ds(t + (PAD - 1), rows), :] for t in starts], axis=0)
        return folded(dot(pair(prior), wc[h]))

    previous = (lax.rem(tm + NX * NY - 1, NX * NY), hd)

    def drive_copy(g):
        rows = chunk_of(g)
        return remote(
            drive.at[:, :, rows], ndrive.at[:, :, rows], nds_sem.at[g], ndr_sem.at[g], previous
        )

    def path_copy(h):
        steps = pl.ds(PAD, T)
        return remote(cur.at[h, steps], ncur.at[h, steps], ncs_sem.at[h], ncr_sem.at[h], previous)

    def start_copy(h):
        return remote(origin.at[h], norigin.at[h], ns_sem.at[h], nr_sem.at[h], previous)

    def gather_chunk(g):
        @pl.when(g == 0)
        def _():
            relay_chunk(0)
            start_own(2)
            relay_chunk(1)

        @pl.when(jnp.logical_and(g > 0, g < NG - 1))
        def _():
            relay_chunk(g + 1)

        @pl.when(g == 1)
        def _():
            start_own(3)

        first = pl.multiple_of(g * L, L)
        starts = [first + b * S for b in range(NB)]
        linear = [linear_of(h, starts, L) for h in range(2)]
        held_chunk(g, 3, far_z, ahead_z).wait_recv()
        for z in range(NZ):
            source = z * 2 + 1 - core
            held_chunk(g, 2, source, partner).wait_recv()
        rows = chunk_of(g)
        total = jnp.zeros((R, 2 * U), F32)
        for s in range(2 * NZ):
            total += dot(xg[s, :, rows, :].reshape(R, 2 * U), inw[s * 2 * U : (s + 1) * 2 * U, :])
        for h in range(2):
            through = total[:, h * U : (h + 1) * U] + bias_ref[h : h + 1, :]
            drive[h, :, rows, :] = through.reshape(NB, L, U)
            curve(h, starts, L, linear[h], through)

        @pl.when(tm > 0)
        def _():
            drive_copy(g).start()

    def compose(h, g):
        first = pl.multiple_of(g * L, L)
        weight = wc[h]
        vector = jnp.where(g == 0, 0.0, vec[h])
        for step in range(L):
            for b in range(NB):
                row = slope[h, pl.ds(first + (b * S + step), 1), :]
                block = leaf.at[h, g, b] if step == 0 else work.at[b]
                product = folded(dot(block[0:U, :], weight)) * row
                out = leaf.at[h, g + 1, b] if step == L - 1 else work.at[b]
                store_pair(out, pl.ds(0, U), product)
            wide = folded(dot(pair(twice(vector)), weight))[0:NB]
            vector = wide * slope[h, pl.ds(first + step, NB, stride=S), :]
            vector = vector + offset[h, pl.ds(first + step, NB, stride=S), :]
        vec[h] = vector
        for b in range(NB):
            repeated = jnp.broadcast_to(vector[b : b + 1, :], (M - U, U))
            store_pair(leaf.at[h, g + 1, b], pl.ds(U, M - U), repeated)

    def row_copy(unit, k):
        return remote(
            mx.at[unit, my_x], mx.at[unit, my_x], mxs_sem.at[unit, k], mxr_sem.at[unit, my_x],
            (my_y * NX + lax.rem(my_x + k, NX), hd),
        )

    def row_arrival(unit, k):
        other = lax.rem(my_x + k, NX)
        return remote(
            mx.at[unit, other], mx.at[unit, other], mxs_sem.at[unit, k], mxr_sem.at[unit, other],
            (my_y * NX + other, hd),
        )

    def state_copy(unit, y):
        return remote(
            leaving.at[unit], entry.at[unit], mys_sem.at[unit], myr_sem.at[unit],
            (lax.rem(y + 1, NY) * NX + my_x, hd),
        )

    def close_slab(h, unit):
        for k in range(4):
            combine(leaf.at[h, NG, 2 * k], leaf.at[h, NG, 2 * k + 1], node1.at[h, k])
        for k in range(2):
            combine(node1.at[h, 2 * k], node1.at[h, 2 * k + 1], node2.at[h, k])
        combine(node2.at[h, 0], node2.at[h, 1], mx.at[unit, my_x])
        for k in range(1, NX):
            row_copy(unit, k).start()

    def close_row(unit):
        for k in range(1, NX):
            row_arrival(unit, k).wait_recv()
        combine(mx.at[unit, 0], mx.at[unit, 1], half.at[0])
        combine(mx.at[unit, 2], mx.at[unit, 3], half.at[1])
        combine(half.at[0], half.at[1], whole)

    def pass_row(h, unit, y):
        @pl.when(my_y == y)
        def _():
            if y == 0:
                entry[unit] = jnp.broadcast_to(init_ref[h : h + 1, :], (16, U))
            else:
                state_copy(unit, y).wait_recv()
            leaving[unit] = apply_map(entry[unit], whole)
            state_copy(unit, y).start()

    def begin(h, unit, last=False):
        @pl.when(my_y == NY - 1)
        def _():
            state_copy(unit, NY - 1).wait_recv()

        fill[0:16, :] = entry[unit]
        for x in range(NX - 1):

            @pl.when(my_x > x)
            def _():
                fill[0:16, :] = apply_map(fill[0:16, :], mx.at[unit, x])

        entering = fill[0:16, :]
        cur[h, PAD - 1 : PAD, :] = entering[0:1]
        starts = [entering]
        for node in (node2.at[h], node1.at[h], leaf.at[h, NG]):
            later = []
            for k in range(len(starts)):
                later.append(starts[k])
                later.append(apply_map(starts[k], node.at[2 * k]))
            starts = later
        states = []
        for b in range(NB):
            states.append(starts[b][0:1])
            for g in range(1, NG):
                states.append(apply_map(starts[b], leaf.at[h, g, b])[0:1])
        state = jnp.concatenate(states, axis=0)
        if last:
            origin[h] = state

            @pl.when(tm > 0)
            def _():
                start_copy(h).start()
                path_copy(h).wait_send()

        return state

    def advance_step(h, state, step, slope, offset, out, base):
        linear = folded(dot(pair(state), wc[h]))
        state = linear * slope[h, pl.ds(step, B, stride=L), :]
        state = state + offset[h, pl.ds(step, B, stride=L), :]
        out[h, pl.ds(base + step, B, stride=L), :] = state
        return state

    def advance(h, state, slope, offset, out, base):
        for step in range(L):
            state = advance_step(h, state, step, slope, offset, out, base)

    def finish(h, unit, last=False):
        advance(h, begin(h, unit, last), slope, offset, cur, PAD)

    def unit_step(u, carry):
        sweep = u // 8
        h = lax.rem(u // 4, 2)
        g = lax.rem(u, 4)

        @pl.when(u < 4)
        def _():
            gather_chunk(g)

        for unit, closes, passes in ((0, 6, (6, 7, 8)), (1, 9, (9, 10, 11)), (2, 13, (13, 14, 15))):

            @pl.when(u == closes)
            def _():
                close_row(unit)

            for y in range(NY - 1):

                @pl.when(u == passes[y])
                def _():
                    pass_row(unit % 2, unit, y)

        @pl.when(jnp.logical_and(g == 0, u >= 8))
        def _():
            finish(h, h)

            @pl.when(tm > 0)
            def _():
                path_copy(h).start()

            ncur[h, PAD - 1 : PAD, :] = cur[h, PAD + T - 1 : PAD + T, :]
            curve(h, [0], T, linear_of(h, [0], T), drive[h].reshape(T, U))

        compose(h, g)

        @pl.when(g == NG - 1)
        def _():
            close_slab(h, sweep * 2 + h)

        return carry

    lax.fori_loop(0, 16, unit_step, 0)

    def out_copy(h):
        return pltpu.make_async_copy(
            cur.at[h, pl.ds(PAD, T)], traj_ref.at[:, pl.ds(h * U, U)], local_sem.at[h]
        )

    def next_copy(h):
        return pltpu.make_async_copy(
            ahead.at[h], next_ref.at[:, pl.ds(h * U, U)], local_sem.at[2 + h]
        )

    def follow(h):
        @pl.when(tm < NX * NY - 1)
        def _():
            start_copy(h).wait_recv()
            advance(h, norigin[h], nslope, noffset, ahead, 0)

        @pl.when(tm == NX * NY - 1)
        def _():
            ahead[h] = jnp.broadcast_to(cur[h, PAD + T - 1 : PAD + T, :], (T, U))

        next_copy(h).start()

    finish(0, 2, last=True)
    out_copy(0).start()

    def following_curve():
        @pl.when(tm < NX * NY - 1)
        def _():
            for g in range(NG):
                drive_copy(g).wait_recv()
            for h in range(2):
                path_copy(h).wait_recv()
                linear = linear_of(h, [0], T, ncur)
                curve(h, [0], T, linear, ndrive[h].reshape(T, U), nslope, noffset)

    close_row(3)

    @pl.when(my_y > 0)
    def _():
        following_curve()

    @pl.when(my_y >= 2)
    def _():
        follow(0)

    for y in range(NY - 1):
        pass_row(1, 3, y)

    @pl.when(my_y == 0)
    def _():
        following_curve()

    @pl.when(my_y < 2)
    def _():
        follow(0)

    state = begin(1, 3, last=True)
    half_way = L // 2
    for step in range(half_way):
        state = advance_step(1, state, step, slope, offset, cur, PAD)

    @pl.when(tm < NX * NY - 1)
    def _():
        start_copy(1).wait_recv()
        own, following = state, norigin[1]
        for step in range(L):
            following = advance_step(1, following, step, nslope, noffset, ahead, 0)
            if half_way + step < L:
                own = advance_step(1, own, half_way + step, slope, offset, cur, PAD)

    @pl.when(tm == NX * NY - 1)
    def _():
        own = state
        for step in range(half_way, L):
            own = advance_step(1, own, step, slope, offset, cur, PAD)
        ahead[1] = jnp.broadcast_to(cur[1, PAD + T - 1 : PAD + T, :], (T, U))

    out_copy(1).start()
    next_copy(1).start()

    def drain(g, carry):
        for kind, to in ((0, ahead_z), (1, back_z), (2, partner)):
            own_chunk(g, kind, to).wait_send()
        held_chunk(g, 3, back_z, ahead_z).wait_send()
        held_chunk(g, 6, back_z, across).wait_send()
        for kind, source in ((4, back_z), (5, ahead_z)):
            held_chunk(g, kind, source, partner).wait_send()
        return carry

    lax.fori_loop(0, NG, drain, 0)

    @pl.when(tm < NX * NY - 1)
    def _():
        edge_copy.wait_send()

    for unit in range(4):
        for k in range(1, NX):
            row_copy(unit, k).wait_send()

        @pl.when(my_y < NY - 1)
        def _():
            state_copy(unit, my_y).wait_send()

    @pl.when(tm > 0)
    def _():
        for g in range(NG):
            drive_copy(g).wait_send()
        for h in range(2):
            start_copy(h).wait_send()

    for h in range(2):
        out_copy(h).wait()
        next_copy(h).wait()


def shards(inputs, in_weight, rec_weight, bias, initial, guess):
    hbm = pl.BlockSpec(memory_space=pltpu.HBM)
    anywhere = pl.BlockSpec(memory_space=pl.ANY)
    out = jax.ShapeDtypeStruct((T, 2 * U), F32)
    dma = pltpu.SemaphoreType.DMA
    results = pl.pallas_call(
        kernel,
        out_shape=(out, out),
        in_specs=[hbm] * 6,
        out_specs=(anywhere, anywhere),
        scratch_shapes=[
            pltpu.VMEM((2, U, U), F32),
            pltpu.VMEM((2, U), F32),
            pltpu.VMEM((2, U), F32),
            pltpu.VMEM((2 * NZ, NB, S, 2 * U), BF16),
            pltpu.VMEM((2 * NZ * 2 * U, 2 * U), BF16),
            pltpu.VMEM((2, 2 * U, 2 * U), BF16),
            pltpu.VMEM((2, PAD + T, U), F32),
            pltpu.VMEM((2, NB, S, U), F32),
            pltpu.VMEM((2, T, U), F32),
            pltpu.VMEM((2, T, U), F32),
            pltpu.VMEM((NB, U, 2 * U), BF16),
            pltpu.VMEM((2, NG + 1, NB, M, 2 * U), BF16),
            pltpu.VMEM((2, 4, M, 2 * U), BF16),
            pltpu.VMEM((2, 2, M, 2 * U), BF16),
            pltpu.VMEM((2, NB, U), F32),
            pltpu.VMEM((4, NX, M, 2 * U), BF16),
            pltpu.VMEM((M, 2 * U), BF16),
            pltpu.VMEM((4, 16, U), F32),
            pltpu.VMEM((4, 16, U), F32),
            pltpu.VMEM((2, M, 2 * U), BF16),
            pltpu.VMEM((8, 2 * U), F32),
            pltpu.VMEM((16, U), F32),
            pltpu.VMEM((2, NB, S, U), F32),
            pltpu.VMEM((2, PAD + T, U), F32),
            pltpu.VMEM((2, T, U), F32),
            pltpu.VMEM((2, T, U), F32),
            pltpu.VMEM((2, B, U), F32),
            pltpu.VMEM((2, B, U), F32),
            pltpu.VMEM((2, T, U), F32),
            dma((7,)),
            dma((7, NG)),
            dma((2 * NZ, NG)),
            dma((4, NX)),
            dma((4, NX)),
            dma((4,)),
            dma((4,)),
            dma((1,)),
            dma((1,)),
            dma((2,)),
            dma((2,)),
            dma((NG,)),
            dma((NG,)),
            dma((2,)),
            dma((2,)),
        ],
        compiler_params=pltpu.CompilerParams(
            collective_id=0, has_side_effects=True, vmem_limit_bytes=56 * 1024 * 1024
        ),
    )(
        inputs.reshape(NB, S, 2 * U),
        in_weight,
        rec_weight,
        bias.reshape(2, U),
        initial.reshape(2, U),
        guess,
    )
    return pl.pallas_call(
        emit,
        out_shape=(out, out),
        in_specs=[anywhere] * 2,
        out_specs=(anywhere, anywhere),
        scratch_shapes=[pltpu.VMEM((2, T, 2 * U), F32), dma((4,)), dma((4,))],
    )(*results)


def emit(a_ref, b_ref, out_a, out_b, held, in_sem, out_sem):
    half = T // 2
    parts = [(k, pl.ds(half * i, half)) for k in range(2) for i in range(2)]
    pairs = ((a_ref, out_a), (b_ref, out_b))
    ins = [
        pltpu.make_async_copy(pairs[k][0].at[rows], held.at[k, rows], in_sem.at[n])
        for n, (k, rows) in enumerate(parts)
    ]
    outs = [
        pltpu.make_async_copy(held.at[k, rows], pairs[k][1].at[rows], out_sem.at[n])
        for n, (k, rows) in enumerate(parts)
    ]
    for copy in ins:
        copy.start()
    for arriving, leaving in zip(ins, outs):
        arriving.wait()
        leaving.start()
    for copy in outs:
        copy.wait()


def solution(mesh):
    in_specs = (
        P("tm", "head"),
        P(None, "head"),
        P("head", None, None),
        P("head"),
        P("head"),
        P("tm", "head"),
    )
    out_specs = (P("tm", "head"), P("tm", "head"))
    return jax.shard_map(
        shards, mesh=mesh, in_specs=in_specs, out_specs=out_specs, check_vma=False
    )
```

```python
import jax
import jax.numpy as jnp
from jax import lax
from jax.experimental import pallas as pl
from jax.experimental.pallas import tpu as pltpu
from jax.sharding import PartitionSpec as P

MESH = pl.DeviceIdType.MESH
F32 = jnp.float32
BF16 = jnp.bfloat16
U = 128
NB = 8
NG = 4
L = 16
S = NG * L
R = NB * L
B = NB * NG
T = NB * S
PAD = 8
M = U + 16
NX = 4
NY = 4
NZ = 4


def split(value):
    high = value.astype(BF16)
    low = (value - high.astype(F32)).astype(BF16)
    return high, low


def pair(value):
    return jnp.concatenate(split(value), axis=1)


def folded(product):
    return product[:, :U] + product[:, U:]


def twice(block):
    return jnp.concatenate([block, block], axis=0)


def dot(a, b):
    return jnp.dot(a, b, preferred_element_type=F32)


def store_pair(ref, rows, value):
    high, low = split(value)
    ref[rows, 0:U] = high
    ref[rows, U : 2 * U] = low


def combine(first, later, out):
    matrix = later[0:U, :]
    product = folded(dot(first[...], twice(matrix)))
    vector = later[U:M, 0:U].astype(F32) + later[U:M, U : 2 * U].astype(F32)
    store_pair(out, pl.ds(0, U), product[0:U])
    store_pair(out, pl.ds(U, M - U), product[U:M] + vector)


def apply_map(state, ref):
    vector = ref[U:M, 0:U].astype(F32) + ref[U:M, U : 2 * U].astype(F32)
    return folded(dot(pair(state), twice(ref[0:U, :]))) + vector


def kernel(
    x_ref, inw_ref, rec_hbm, bias_hbm, init_hbm, guess_ref,
    traj_ref, next_ref,
    rec_ref, bias_ref, init_ref, xg, inw, wc, cur, drive, slope, offset, work, leaf, node1, node2, vec, mx, whole, entry, leaving, half, edge, fill,
    ndrive, ncur, nslope, noffset, origin, norigin, ahead,
    local_sem, xs_sem, xr_sem, mxs_sem, mxr_sem, mys_sem, myr_sem, es_sem, er_sem, ns_sem, nr_sem,
    nds_sem, ndr_sem, ncs_sem, ncr_sem,
):
    tm = lax.axis_index("tm")
    hd = lax.axis_index("head")
    my_x = lax.rem(tm, NX)
    my_y = tm // NX
    my_z = hd // 2
    core = lax.rem(hd, 2)
    turn = 1 - 2 * core
    partner = my_z * 2 + 1 - core
    ahead_z = lax.rem(my_z + turn + NZ, NZ) * 2 + core
    back_z = lax.rem(my_z - turn + NZ, NZ) * 2 + core
    far_z = lax.rem(my_z + 2, NZ) * 2 + core
    across = ahead_z + turn

    def remote(src, dst, ssem, rsem, to):
        return pltpu.make_async_remote_copy(
            src_ref=src, dst_ref=dst, send_sem=ssem, recv_sem=rsem, device_id=to, device_id_type=MESH
        )

    guess_in = [
        pltpu.make_async_copy(
            guess_ref.at[:, pl.ds(h * U, U)], cur.at[h, pl.ds(PAD, T)], local_sem.at[h]
        )
        for h in range(2)
    ]
    weight_in = pltpu.make_async_copy(inw_ref, inw, local_sem.at[2])
    own_in = pltpu.make_async_copy(x_ref, xg.at[hd], local_sem.at[3])
    small_in = [
        pltpu.make_async_copy(src, dst, local_sem.at[4 + k])
        for k, (src, dst) in enumerate(
            ((rec_hbm, rec_ref), (bias_hbm, bias_ref), (init_hbm, init_ref))
        )
    ]
    for copy in small_in:
        copy.start()
    own_in.start()
    weight_in.start()
    for copy in guess_in:
        copy.start()

    barrier = pltpu.get_barrier_semaphore()

    def greet(a, b):
        pl.semaphore_signal(barrier, inc=1, device_id=(a, b), device_id_type=MESH)

    greet(tm, partner)
    greet(tm, ahead_z)
    greet(tm, back_z)
    greet(tm, across)
    for k in range(1, NX):
        greet(my_y * NX + lax.rem(my_x + k, NX), hd)
    for k in range(1, NY):
        greet(lax.rem(my_y + k, NY) * NX + my_x, hd)
    turns_up = jnp.logical_and(my_x == NX - 1, my_y < NY - 1)
    turns_down = jnp.logical_and(my_x == 0, my_y > 0)

    @pl.when(turns_up)
    def _():
        greet(tm + 1, hd)

    @pl.when(turns_down)
    def _():
        greet(tm - 1, hd)

    turning = jnp.logical_or(turns_up, turns_down).astype(jnp.int32)
    pl.semaphore_wait(barrier, 4 + NX - 1 + NY - 1 + turning)

    def chunk_of(g):
        return pl.ds(pl.multiple_of(g * L, L), L)

    def own_chunk(g, kind, to):
        rows = chunk_of(g)
        return remote(
            x_ref.at[:, rows], xg.at[hd, :, rows], xs_sem.at[kind, g], xr_sem.at[hd, g], (tm, to)
        )

    def held_chunk(g, kind, source, to):
        rows = chunk_of(g)
        return remote(
            xg.at[source, :, rows], xg.at[source, :, rows], xs_sem.at[kind, g], xr_sem.at[source, g], (tm, to)
        )

    def start_own(g):
        own_chunk(g, 0, ahead_z).start()
        own_chunk(g, 1, back_z).start()
        own_chunk(g, 2, partner).start()

    start_own(0)
    start_own(1)

    edge_copy = remote(
        guess_ref.at[pl.ds(T - 8, 8), :], edge, es_sem.at[0], er_sem.at[0],
        (lax.rem(tm + 1, NX * NY), hd),
    )

    @pl.when(tm < NX * NY - 1)
    def _():
        edge_copy.start()

    for copy in small_in:
        copy.wait()

    for h in range(2):
        transposed = rec_ref[h].T
        high, low = split(transposed)
        for k in range(2):
            wc[h, pl.ds(k * U, U), 0:U] = high
            wc[h, pl.ds(k * U, U), U : 2 * U] = low

    row_id = lax.broadcasted_iota(jnp.int32, (U, U), 0)
    identity = jnp.where(row_id == lax.broadcasted_iota(jnp.int32, (U, U), 1), 1.0, 0.0)
    for h in range(2):
        for b in range(NB):
            store_pair(leaf.at[h, 0, b], pl.ds(0, U), identity)

    for copy in guess_in:
        copy.wait()

    @pl.when(tm == 0)
    def _():
        for h in range(2):
            cur[h, PAD - 1 : PAD, :] = init_ref[h : h + 1, :]

    @pl.when(tm > 0)
    def _():
        edge_copy.wait_recv()
        for h in range(2):
            cur[h, PAD - 1 : PAD, :] = edge[7:8, h * U : (h + 1) * U]

    own_in.wait()
    weight_in.wait()

    def relay_chunk(g):
        held_chunk(g, 3, back_z, ahead_z).wait_recv()
        held_chunk(g, 3, back_z, ahead_z).start()
        held_chunk(g, 6, back_z, across).start()
        held_chunk(g, 4, back_z, partner).start()
        held_chunk(g, 5, ahead_z, partner).wait_recv()
        held_chunk(g, 5, ahead_z, partner).start()

    def curve(h, starts, rows, linear, through, slope=slope, offset=offset):
        value = jnp.tanh(linear + through)
        steep = 1.0 - value * value
        rest = value - steep * linear
        for k, t in enumerate(starts):
            slope[h, pl.ds(t, rows), :] = steep[k * rows : (k + 1) * rows]
            offset[h, pl.ds(t, rows), :] = rest[k * rows : (k + 1) * rows]

    def linear_of(h, starts, rows, cur=cur):
        prior = jnp.concatenate([cur[h, pl.ds(t + (PAD - 1), rows), :] for t in starts], axis=0)
        return folded(dot(pair(prior), wc[h]))

    previous = (lax.rem(tm + NX * NY - 1, NX * NY), hd)

    def drive_copy(g):
        rows = chunk_of(g)
        return remote(
            drive.at[:, :, rows], ndrive.at[:, :, rows], nds_sem.at[g], ndr_sem.at[g], previous
        )

    def path_copy(h):
        steps = pl.ds(PAD, T)
        return remote(cur.at[h, steps], ncur.at[h, steps], ncs_sem.at[h], ncr_sem.at[h], previous)

    def start_copy(h):
        return remote(origin.at[h], norigin.at[h], ns_sem.at[h], nr_sem.at[h], previous)

    def gather_chunk(g):
        @pl.when(g == 0)
        def _():
            relay_chunk(0)
            start_own(2)
            relay_chunk(1)

        @pl.when(jnp.logical_and(g > 0, g < NG - 1))
        def _():
            relay_chunk(g + 1)

        @pl.when(g == 1)
        def _():
            start_own(3)

        first = pl.multiple_of(g * L, L)
        starts = [first + b * S for b in range(NB)]
        linear = [linear_of(h, starts, L) for h in range(2)]
        held_chunk(g, 3, far_z, ahead_z).wait_recv()
        for z in range(NZ):
            source = z * 2 + 1 - core
            held_chunk(g, 2, source, partner).wait_recv()
        rows = chunk_of(g)
        total = jnp.zeros((R, 2 * U), F32)
        for s in range(2 * NZ):
            total += dot(xg[s, :, rows, :].reshape(R, 2 * U), inw[s * 2 * U : (s + 1) * 2 * U, :])
        for h in range(2):
            through = total[:, h * U : (h + 1) * U] + bias_ref[h : h + 1, :]
            drive[h, :, rows, :] = through.reshape(NB, L, U)
            curve(h, starts, L, linear[h], through)

        @pl.when(tm > 0)
        def _():
            drive_copy(g).start()

    def compose(h, g):
        first = pl.multiple_of(g * L, L)
        weight = wc[h]
        vector = jnp.where(g == 0, 0.0, vec[h])
        for step in range(L):
            for lead in range(0, NB, 2):
                both = (lead, lead + 1)
                blocks = [leaf.at[h, g, b] if step == 0 else work.at[b] for b in both]
                left = [block[0:U, :] for block in blocks]
                if lead == NB - 2:
                    left.append(pair(twice(vector)))
                product = folded(dot(jnp.concatenate(left, axis=0), weight))
                for k, b in enumerate(both):
                    row = slope[h, pl.ds(first + (b * S + step), 1), :]
                    out = leaf.at[h, g + 1, b] if step == L - 1 else work.at[b]
                    store_pair(out, pl.ds(0, U), product[k * U : (k + 1) * U] * row)
            wide = product[2 * U : 2 * U + NB]
            vector = wide * slope[h, pl.ds(first + step, NB, stride=S), :]
            vector = vector + offset[h, pl.ds(first + step, NB, stride=S), :]
        vec[h] = vector
        for b in range(NB):
            repeated = jnp.broadcast_to(vector[b : b + 1, :], (M - U, U))
            store_pair(leaf.at[h, g + 1, b], pl.ds(U, M - U), repeated)

    def row_copy(unit, k):
        return remote(
            mx.at[unit, my_x], mx.at[unit, my_x], mxs_sem.at[unit, k], mxr_sem.at[unit, my_x],
            (my_y * NX + lax.rem(my_x + k, NX), hd),
        )

    def row_arrival(unit, k):
        other = lax.rem(my_x + k, NX)
        return remote(
            mx.at[unit, other], mx.at[unit, other], mxs_sem.at[unit, k], mxr_sem.at[unit, other],
            (my_y * NX + other, hd),
        )

    def state_copy(unit, y):
        return remote(
            leaving.at[unit], entry.at[unit], mys_sem.at[unit], myr_sem.at[unit],
            (lax.rem(y + 1, NY) * NX + my_x, hd),
        )

    def close_slab(h, unit):
        for k in range(4):
            combine(leaf.at[h, NG, 2 * k], leaf.at[h, NG, 2 * k + 1], node1.at[h, k])
        for k in range(2):
            combine(node1.at[h, 2 * k], node1.at[h, 2 * k + 1], node2.at[h, k])
        combine(node2.at[h, 0], node2.at[h, 1], mx.at[unit, my_x])
        for k in range(1, NX):
            row_copy(unit, k).start()

    def close_row(unit):
        for k in range(1, NX):
            row_arrival(unit, k).wait_recv()
        combine(mx.at[unit, 0], mx.at[unit, 1], half.at[0])
        combine(mx.at[unit, 2], mx.at[unit, 3], half.at[1])
        combine(half.at[0], half.at[1], whole)

    def pass_row(h, unit, y):
        @pl.when(my_y == y)
        def _():
            if y == 0:
                entry[unit] = jnp.broadcast_to(init_ref[h : h + 1, :], (16, U))
            else:
                state_copy(unit, y).wait_recv()
            leaving[unit] = apply_map(entry[unit], whole)
            state_copy(unit, y).start()

    def begin(h, unit, last=False):
        @pl.when(my_y == NY - 1)
        def _():
            state_copy(unit, NY - 1).wait_recv()

        fill[0:16, :] = entry[unit]
        for x in range(NX - 1):

            @pl.when(my_x > x)
            def _():
                fill[0:16, :] = apply_map(fill[0:16, :], mx.at[unit, x])

        entering = fill[0:16, :]
        cur[h, PAD - 1 : PAD, :] = entering[0:1]
        starts = [entering]
        for node in (node2.at[h], node1.at[h], leaf.at[h, NG]):
            later = []
            for k in range(len(starts)):
                later.append(starts[k])
                later.append(apply_map(starts[k], node.at[2 * k]))
            starts = later
        states = []
        for b in range(NB):
            states.append(starts[b][0:1])
            for g in range(1, NG):
                states.append(apply_map(starts[b], leaf.at[h, g, b])[0:1])
        state = jnp.concatenate(states, axis=0)
        if last:
            origin[h] = state

            @pl.when(tm > 0)
            def _():
                start_copy(h).start()
                path_copy(h).wait_send()

        return state

    def advance_step(h, state, step, slope, offset, out, base):
        linear = folded(dot(pair(state), wc[h]))
        state = linear * slope[h, pl.ds(step, B, stride=L), :]
        state = state + offset[h, pl.ds(step, B, stride=L), :]
        out[h, pl.ds(base + step, B, stride=L), :] = state
        return state

    def advance(h, state, slope, offset, out, base):
        for step in range(L):
            state = advance_step(h, state, step, slope, offset, out, base)

    def finish(h, unit, last=False):
        advance(h, begin(h, unit, last), slope, offset, cur, PAD)

    def unit_step(u, carry):
        sweep = u // 8
        h = lax.rem(u // 4, 2)
        g = lax.rem(u, 4)

        @pl.when(u < 4)
        def _():
            gather_chunk(g)

        for unit, closes, passes in ((0, 6, (6, 7, 8)), (1, 9, (9, 10, 11)), (2, 13, (13, 14, 15))):

            @pl.when(u == closes)
            def _():
                close_row(unit)

            for y in range(NY - 1):

                @pl.when(u == passes[y])
                def _():
                    pass_row(unit % 2, unit, y)

        @pl.when(jnp.logical_and(g == 0, u >= 8))
        def _():
            finish(h, h)

            @pl.when(tm > 0)
            def _():
                path_copy(h).start()

            ncur[h, PAD - 1 : PAD, :] = cur[h, PAD + T - 1 : PAD + T, :]
            curve(h, [0], T, linear_of(h, [0], T), drive[h].reshape(T, U))

        compose(h, g)

        @pl.when(g == NG - 1)
        def _():
            close_slab(h, sweep * 2 + h)

        return carry

    lax.fori_loop(0, 16, unit_step, 0)

    def out_copy(h):
        return pltpu.make_async_copy(
            cur.at[h, pl.ds(PAD, T)], traj_ref.at[:, pl.ds(h * U, U)], local_sem.at[h]
        )

    def next_copy(h):
        return pltpu.make_async_copy(
            ahead.at[h], next_ref.at[:, pl.ds(h * U, U)], local_sem.at[2 + h]
        )

    def follow(h):
        @pl.when(tm < NX * NY - 1)
        def _():
            start_copy(h).wait_recv()
            advance(h, norigin[h], nslope, noffset, ahead, 0)

        @pl.when(tm == NX * NY - 1)
        def _():
            ahead[h] = jnp.broadcast_to(cur[h, PAD + T - 1 : PAD + T, :], (T, U))

        next_copy(h).start()

    finish(0, 2, last=True)
    out_copy(0).start()

    def following_curve():
        @pl.when(tm < NX * NY - 1)
        def _():
            for g in range(NG):
                drive_copy(g).wait_recv()
            for h in range(2):
                path_copy(h).wait_recv()
                linear = linear_of(h, [0], T, ncur)
                curve(h, [0], T, linear, ndrive[h].reshape(T, U), nslope, noffset)

    close_row(3)

    @pl.when(my_y > 0)
    def _():
        following_curve()

    @pl.when(my_y >= 2)
    def _():
        follow(0)

    for y in range(NY - 1):
        pass_row(1, 3, y)

    @pl.when(my_y == 0)
    def _():
        following_curve()

    @pl.when(my_y < 2)
    def _():
        follow(0)

    state = begin(1, 3, last=True)
    half_way = L // 2
    for step in range(half_way):
        state = advance_step(1, state, step, slope, offset, cur, PAD)

    @pl.when(tm < NX * NY - 1)
    def _():
        start_copy(1).wait_recv()
        own, following = state, norigin[1]
        for step in range(L):
            following = advance_step(1, following, step, nslope, noffset, ahead, 0)
            if half_way + step < L:
                own = advance_step(1, own, half_way + step, slope, offset, cur, PAD)

    @pl.when(tm == NX * NY - 1)
    def _():
        own = state
        for step in range(half_way, L):
            own = advance_step(1, own, step, slope, offset, cur, PAD)
        ahead[1] = jnp.broadcast_to(cur[1, PAD + T - 1 : PAD + T, :], (T, U))

    out_copy(1).start()
    next_copy(1).start()

    def drain(g, carry):
        for kind, to in ((0, ahead_z), (1, back_z), (2, partner)):
            own_chunk(g, kind, to).wait_send()
        held_chunk(g, 3, back_z, ahead_z).wait_send()
        held_chunk(g, 6, back_z, across).wait_send()
        for kind, source in ((4, back_z), (5, ahead_z)):
            held_chunk(g, kind, source, partner).wait_send()
        return carry

    lax.fori_loop(0, NG, drain, 0)

    @pl.when(tm < NX * NY - 1)
    def _():
        edge_copy.wait_send()

    for unit in range(4):
        for k in range(1, NX):
            row_copy(unit, k).wait_send()

        @pl.when(my_y < NY - 1)
        def _():
            state_copy(unit, my_y).wait_send()

    @pl.when(tm > 0)
    def _():
        for g in range(NG):
            drive_copy(g).wait_send()
        for h in range(2):
            start_copy(h).wait_send()

    for h in range(2):
        out_copy(h).wait()
        next_copy(h).wait()


def shards(inputs, in_weight, rec_weight, bias, initial, guess):
    hbm = pl.BlockSpec(memory_space=pltpu.HBM)
    anywhere = pl.BlockSpec(memory_space=pl.ANY)
    out = jax.ShapeDtypeStruct((T, 2 * U), F32)
    dma = pltpu.SemaphoreType.DMA
    results = pl.pallas_call(
        kernel,
        out_shape=(out, out),
        in_specs=[hbm] * 6,
        out_specs=(anywhere, anywhere),
        scratch_shapes=[
            pltpu.VMEM((2, U, U), F32),
            pltpu.VMEM((2, U), F32),
            pltpu.VMEM((2, U), F32),
            pltpu.VMEM((2 * NZ, NB, S, 2 * U), BF16),
            pltpu.VMEM((2 * NZ * 2 * U, 2 * U), BF16),
            pltpu.VMEM((2, 2 * U, 2 * U), BF16),
            pltpu.VMEM((2, PAD + T, U), F32),
            pltpu.VMEM((2, NB, S, U), F32),
            pltpu.VMEM((2, T, U), F32),
            pltpu.VMEM((2, T, U), F32),
            pltpu.VMEM((NB, U, 2 * U), BF16),
            pltpu.VMEM((2, NG + 1, NB, M, 2 * U), BF16),
            pltpu.VMEM((2, 4, M, 2 * U), BF16),
            pltpu.VMEM((2, 2, M, 2 * U), BF16),
            pltpu.VMEM((2, NB, U), F32),
            pltpu.VMEM((4, NX, M, 2 * U), BF16),
            pltpu.VMEM((M, 2 * U), BF16),
            pltpu.VMEM((4, 16, U), F32),
            pltpu.VMEM((4, 16, U), F32),
            pltpu.VMEM((2, M, 2 * U), BF16),
            pltpu.VMEM((8, 2 * U), F32),
            pltpu.VMEM((16, U), F32),
            pltpu.VMEM((2, NB, S, U), F32),
            pltpu.VMEM((2, PAD + T, U), F32),
            pltpu.VMEM((2, T, U), F32),
            pltpu.VMEM((2, T, U), F32),
            pltpu.VMEM((2, B, U), F32),
            pltpu.VMEM((2, B, U), F32),
            pltpu.VMEM((2, T, U), F32),
            dma((7,)),
            dma((7, NG)),
            dma((2 * NZ, NG)),
            dma((4, NX)),
            dma((4, NX)),
            dma((4,)),
            dma((4,)),
            dma((1,)),
            dma((1,)),
            dma((2,)),
            dma((2,)),
            dma((NG,)),
            dma((NG,)),
            dma((2,)),
            dma((2,)),
        ],
        compiler_params=pltpu.CompilerParams(
            collective_id=0, has_side_effects=True, vmem_limit_bytes=56 * 1024 * 1024
        ),
    )(
        inputs.reshape(NB, S, 2 * U),
        in_weight,
        rec_weight,
        bias.reshape(2, U),
        initial.reshape(2, U),
        guess,
    )
    return pl.pallas_call(
        emit,
        out_shape=(out, out),
        in_specs=[anywhere] * 2,
        out_specs=(anywhere, anywhere),
        scratch_shapes=[pltpu.VMEM((2, T, 2 * U), F32), dma((4,)), dma((4,))],
    )(*results)


def emit(a_ref, b_ref, out_a, out_b, held, in_sem, out_sem):
    half = T // 2
    parts = [(k, pl.ds(half * i, half)) for k in range(2) for i in range(2)]
    pairs = ((a_ref, out_a), (b_ref, out_b))
    ins = [
        pltpu.make_async_copy(pairs[k][0].at[rows], held.at[k, rows], in_sem.at[n])
        for n, (k, rows) in enumerate(parts)
    ]
    outs = [
        pltpu.make_async_copy(held.at[k, rows], pairs[k][1].at[rows], out_sem.at[n])
        for n, (k, rows) in enumerate(parts)
    ]
    for copy in ins:
        copy.start()
    for arriving, leaving in zip(ins, outs):
        arriving.wait()
        leaving.start()
    for copy in outs:
        copy.wait()


def solution(mesh):
    in_specs = (
        P("tm", "head"),
        P(None, "head"),
        P("head", None, None),
        P("head"),
        P("head"),
        P("tm", "head"),
    )
    out_specs = (P("tm", "head"), P("tm", "head"))
    return jax.shard_map(
        shards, mesh=mesh, in_specs=in_specs, out_specs=out_specs, check_vma=False
    )
```

```python
import jax
import jax.numpy as jnp
from jax import lax
from jax.experimental import pallas as pl
from jax.experimental.pallas import tpu as pltpu
from jax.sharding import PartitionSpec as P

MESH = pl.DeviceIdType.MESH
F32 = jnp.float32
BF16 = jnp.bfloat16
U = 128
NB = 8
NG = 4
L = 16
S = NG * L
R = NB * L
B = NB * NG
T = NB * S
PAD = 8
M = U + 16
NX = 4
NY = 4
NZ = 4


def split(value):
    high = value.astype(BF16)
    low = (value - high.astype(F32)).astype(BF16)
    return high, low


def pair(value):
    return jnp.concatenate(split(value), axis=1)


def folded(product):
    return product[:, :U] + product[:, U:]


def twice(block):
    return jnp.concatenate([block, block], axis=0)


def dot(a, b):
    return jnp.dot(a, b, preferred_element_type=F32)


def store_pair(ref, rows, value):
    high, low = split(value)
    ref[rows, 0:U] = high
    ref[rows, U : 2 * U] = low


def combine(first, later, out):
    matrix = later[0:U, :]
    product = folded(dot(first[...], twice(matrix)))
    vector = later[U:M, 0:U].astype(F32) + later[U:M, U : 2 * U].astype(F32)
    store_pair(out, pl.ds(0, U), product[0:U])
    store_pair(out, pl.ds(U, M - U), product[U:M] + vector)


def apply_map(state, ref):
    vector = ref[U:M, 0:U].astype(F32) + ref[U:M, U : 2 * U].astype(F32)
    return folded(dot(pair(state), twice(ref[0:U, :]))) + vector


def kernel(
    x_ref, inw_ref, rec_hbm, bias_hbm, init_hbm, guess_ref,
    traj_ref, next_ref,
    rec_ref, bias_ref, init_ref, xg, inw, wc, cur, drive, slope, offset, work, leaf, node1, node2, vec, mx, whole, entry, leaving, half, edge, fill,
    ndrive, ncur, nslope, noffset, origin, norigin, ahead,
    local_sem, xs_sem, xr_sem, mxs_sem, mxr_sem, mys_sem, myr_sem, es_sem, er_sem, ns_sem, nr_sem,
    nds_sem, ndr_sem, ncs_sem, ncr_sem,
):
    tm = lax.axis_index("tm")
    hd = lax.axis_index("head")
    my_x = lax.rem(tm, NX)
    my_y = tm // NX
    my_z = hd // 2
    core = lax.rem(hd, 2)
    turn = 1 - 2 * core
    partner = my_z * 2 + 1 - core
    ahead_z = lax.rem(my_z + turn + NZ, NZ) * 2 + core
    back_z = lax.rem(my_z - turn + NZ, NZ) * 2 + core
    far_z = lax.rem(my_z + 2, NZ) * 2 + core
    across = ahead_z + turn

    def remote(src, dst, ssem, rsem, to):
        return pltpu.make_async_remote_copy(
            src_ref=src, dst_ref=dst, send_sem=ssem, recv_sem=rsem, device_id=to, device_id_type=MESH
        )

    guess_in = [
        pltpu.make_async_copy(
            guess_ref.at[:, pl.ds(h * U, U)], cur.at[h, pl.ds(PAD, T)], local_sem.at[h]
        )
        for h in range(2)
    ]
    weight_in = pltpu.make_async_copy(inw_ref, inw, local_sem.at[2])
    own_in = pltpu.make_async_copy(x_ref, xg.at[hd], local_sem.at[3])
    small_in = [
        pltpu.make_async_copy(src, dst, local_sem.at[4 + k])
        for k, (src, dst) in enumerate(
            ((rec_hbm, rec_ref), (bias_hbm, bias_ref), (init_hbm, init_ref))
        )
    ]
    for copy in small_in:
        copy.start()
    own_in.start()
    weight_in.start()
    for copy in guess_in:
        copy.start()

    barrier = pltpu.get_barrier_semaphore()

    def greet(a, b):
        pl.semaphore_signal(barrier, inc=1, device_id=(a, b), device_id_type=MESH)

    greet(tm, partner)
    greet(tm, ahead_z)
    greet(tm, back_z)
    greet(tm, across)
    for k in range(1, NX):
        greet(my_y * NX + lax.rem(my_x + k, NX), hd)
    for k in range(1, NY):
        greet(lax.rem(my_y + k, NY) * NX + my_x, hd)
    turns_up = jnp.logical_and(my_x == NX - 1, my_y < NY - 1)
    turns_down = jnp.logical_and(my_x == 0, my_y > 0)

    @pl.when(turns_up)
    def _():
        greet(tm + 1, hd)

    @pl.when(turns_down)
    def _():
        greet(tm - 1, hd)

    turning = jnp.logical_or(turns_up, turns_down).astype(jnp.int32)
    pl.semaphore_wait(barrier, 4 + NX - 1 + NY - 1 + turning)

    def chunk_of(g):
        return pl.ds(pl.multiple_of(g * L, L), L)

    def own_chunk(g, kind, to):
        rows = chunk_of(g)
        return remote(
            x_ref.at[:, rows], xg.at[hd, :, rows], xs_sem.at[kind, g], xr_sem.at[hd, g], (tm, to)
        )

    def held_chunk(g, kind, source, to):
        rows = chunk_of(g)
        return remote(
            xg.at[source, :, rows], xg.at[source, :, rows], xs_sem.at[kind, g], xr_sem.at[source, g], (tm, to)
        )

    def start_own(g):
        own_chunk(g, 0, ahead_z).start()
        own_chunk(g, 1, back_z).start()
        own_chunk(g, 2, partner).start()

    start_own(0)
    start_own(1)

    edge_copy = remote(
        guess_ref.at[pl.ds(T - 8, 8), :], edge, es_sem.at[0], er_sem.at[0],
        (lax.rem(tm + 1, NX * NY), hd),
    )

    @pl.when(tm < NX * NY - 1)
    def _():
        edge_copy.start()

    for copy in small_in:
        copy.wait()

    for h in range(2):
        transposed = rec_ref[h].T
        high, low = split(transposed)
        for k in range(2):
            wc[h, pl.ds(k * U, U), 0:U] = high
            wc[h, pl.ds(k * U, U), U : 2 * U] = low

    row_id = lax.broadcasted_iota(jnp.int32, (U, U), 0)
    identity = jnp.where(row_id == lax.broadcasted_iota(jnp.int32, (U, U), 1), 1.0, 0.0)
    for h in range(2):
        for b in range(NB):
            store_pair(leaf.at[h, 0, b], pl.ds(0, U), identity)

    for copy in guess_in:
        copy.wait()

    @pl.when(tm == 0)
    def _():
        for h in range(2):
            cur[h, PAD - 1 : PAD, :] = init_ref[h : h + 1, :]

    @pl.when(tm > 0)
    def _():
        edge_copy.wait_recv()
        for h in range(2):
            cur[h, PAD - 1 : PAD, :] = edge[7:8, h * U : (h + 1) * U]

    own_in.wait()
    weight_in.wait()

    def relay_chunk(g):
        held_chunk(g, 3, back_z, ahead_z).wait_recv()
        held_chunk(g, 3, back_z, ahead_z).start()
        held_chunk(g, 6, back_z, across).start()
        held_chunk(g, 4, back_z, partner).start()
        held_chunk(g, 5, ahead_z, partner).wait_recv()
        held_chunk(g, 5, ahead_z, partner).start()

    def curve(h, starts, rows, linear, through, slope=slope, offset=offset):
        value = jnp.tanh(linear + through)
        steep = 1.0 - value * value
        rest = value - steep * linear
        for k, t in enumerate(starts):
            slope[h, pl.ds(t, rows), :] = steep[k * rows : (k + 1) * rows]
            offset[h, pl.ds(t, rows), :] = rest[k * rows : (k + 1) * rows]

    def linear_of(h, starts, rows, cur=cur):
        prior = jnp.concatenate([cur[h, pl.ds(t + (PAD - 1), rows), :] for t in starts], axis=0)
        return folded(dot(pair(prior), wc[h]))

    previous = (lax.rem(tm + NX * NY - 1, NX * NY), hd)

    def drive_copy(g):
        rows = chunk_of(g)
        return remote(
            drive.at[:, :, rows], ndrive.at[:, :, rows], nds_sem.at[g], ndr_sem.at[g], previous
        )

    def path_copy(h):
        steps = pl.ds(PAD, T)
        return remote(cur.at[h, steps], ncur.at[h, steps], ncs_sem.at[h], ncr_sem.at[h], previous)

    def start_copy(h):
        return remote(origin.at[h], norigin.at[h], ns_sem.at[h], nr_sem.at[h], previous)

    def gather_chunk(g):
        @pl.when(g == 0)
        def _():
            relay_chunk(0)
            start_own(2)
            relay_chunk(1)

        @pl.when(jnp.logical_and(g > 0, g < NG - 1))
        def _():
            relay_chunk(g + 1)

        @pl.when(g == 1)
        def _():
            start_own(3)

        first = pl.multiple_of(g * L, L)
        starts = [first + b * S for b in range(NB)]
        linear = [linear_of(h, starts, L) for h in range(2)]
        held_chunk(g, 3, far_z, ahead_z).wait_recv()
        for z in range(NZ):
            source = z * 2 + 1 - core
            held_chunk(g, 2, source, partner).wait_recv()
        rows = chunk_of(g)
        total = jnp.zeros((R, 2 * U), F32)
        for s in range(2 * NZ):
            total += dot(xg[s, :, rows, :].reshape(R, 2 * U), inw[s * 2 * U : (s + 1) * 2 * U, :])
        for h in range(2):
            through = total[:, h * U : (h + 1) * U] + bias_ref[h : h + 1, :]
            drive[h, :, rows, :] = through.reshape(NB, L, U)
            curve(h, starts, L, linear[h], through)

        @pl.when(tm > 0)
        def _():
            drive_copy(g).start()

    def compose(h, g):
        first = pl.multiple_of(g * L, L)
        weight = wc[h]
        vector = jnp.where(g == 0, 0.0, vec[h])
        for step in range(L):
            for lead in range(0, NB, 4):
                both = range(lead, lead + 4)
                blocks = [leaf.at[h, g, b] if step == 0 else work.at[b] for b in both]
                left = [block[0:U, :] for block in blocks]
                if lead == NB - 4:
                    left.append(pair(twice(vector)))
                product = folded(dot(jnp.concatenate(left, axis=0), weight))
                for k, b in enumerate(both):
                    row = slope[h, pl.ds(first + (b * S + step), 1), :]
                    out = leaf.at[h, g + 1, b] if step == L - 1 else work.at[b]
                    store_pair(out, pl.ds(0, U), product[k * U : (k + 1) * U] * row)
            wide = product[4 * U : 4 * U + NB]
            vector = wide * slope[h, pl.ds(first + step, NB, stride=S), :]
            vector = vector + offset[h, pl.ds(first + step, NB, stride=S), :]
        vec[h] = vector
        for b in range(NB):
            repeated = jnp.broadcast_to(vector[b : b + 1, :], (M - U, U))
            store_pair(leaf.at[h, g + 1, b], pl.ds(U, M - U), repeated)

    def row_copy(unit, k):
        return remote(
            mx.at[unit, my_x], mx.at[unit, my_x], mxs_sem.at[unit, k], mxr_sem.at[unit, my_x],
            (my_y * NX + lax.rem(my_x + k, NX), hd),
        )

    def row_arrival(unit, k):
        other = lax.rem(my_x + k, NX)
        return remote(
            mx.at[unit, other], mx.at[unit, other], mxs_sem.at[unit, k], mxr_sem.at[unit, other],
            (my_y * NX + other, hd),
        )

    def state_copy(unit, y):
        return remote(
            leaving.at[unit], entry.at[unit], mys_sem.at[unit], myr_sem.at[unit],
            (lax.rem(y + 1, NY) * NX + my_x, hd),
        )

    def close_slab(h, unit):
        for k in range(4):
            combine(leaf.at[h, NG, 2 * k], leaf.at[h, NG, 2 * k + 1], node1.at[h, k])
        for k in range(2):
            combine(node1.at[h, 2 * k], node1.at[h, 2 * k + 1], node2.at[h, k])
        combine(node2.at[h, 0], node2.at[h, 1], mx.at[unit, my_x])
        for k in range(1, NX):
            row_copy(unit, k).start()

    def close_row(unit):
        for k in range(1, NX):
            row_arrival(unit, k).wait_recv()
        combine(mx.at[unit, 0], mx.at[unit, 1], half.at[0])
        combine(mx.at[unit, 2], mx.at[unit, 3], half.at[1])
        combine(half.at[0], half.at[1], whole)

    def pass_row(h, unit, y):
        @pl.when(my_y == y)
        def _():
            if y == 0:
                entry[unit] = jnp.broadcast_to(init_ref[h : h + 1, :], (16, U))
            else:
                state_copy(unit, y).wait_recv()
            leaving[unit] = apply_map(entry[unit], whole)
            state_copy(unit, y).start()

    def begin(h, unit, last=False):
        @pl.when(my_y == NY - 1)
        def _():
            state_copy(unit, NY - 1).wait_recv()

        fill[0:16, :] = entry[unit]
        for x in range(NX - 1):

            @pl.when(my_x > x)
            def _():
                fill[0:16, :] = apply_map(fill[0:16, :], mx.at[unit, x])

        entering = fill[0:16, :]
        cur[h, PAD - 1 : PAD, :] = entering[0:1]
        starts = [entering]
        for node in (node2.at[h], node1.at[h], leaf.at[h, NG]):
            later = []
            for k in range(len(starts)):
                later.append(starts[k])
                later.append(apply_map(starts[k], node.at[2 * k]))
            starts = later
        states = []
        for b in range(NB):
            states.append(starts[b][0:1])
            for g in range(1, NG):
                states.append(apply_map(starts[b], leaf.at[h, g, b])[0:1])
        state = jnp.concatenate(states, axis=0)
        if last:
            origin[h] = state

            @pl.when(tm > 0)
            def _():
                start_copy(h).start()
                path_copy(h).wait_send()

        return state

    def advance_step(h, state, step, slope, offset, out, base):
        linear = folded(dot(pair(state), wc[h]))
        state = linear * slope[h, pl.ds(step, B, stride=L), :]
        state = state + offset[h, pl.ds(step, B, stride=L), :]
        out[h, pl.ds(base + step, B, stride=L), :] = state
        return state

    def advance(h, state, slope, offset, out, base):
        for step in range(L):
            state = advance_step(h, state, step, slope, offset, out, base)

    def finish(h, unit, last=False):
        advance(h, begin(h, unit, last), slope, offset, cur, PAD)

    def unit_step(u, carry):
        sweep = u // 8
        h = lax.rem(u // 4, 2)
        g = lax.rem(u, 4)

        @pl.when(u < 4)
        def _():
            gather_chunk(g)

        for unit, closes, passes in ((0, 6, (6, 7, 8)), (1, 9, (9, 10, 11)), (2, 13, (13, 14, 15))):

            @pl.when(u == closes)
            def _():
                close_row(unit)

            for y in range(NY - 1):

                @pl.when(u == passes[y])
                def _():
                    pass_row(unit % 2, unit, y)

        @pl.when(jnp.logical_and(g == 0, u >= 8))
        def _():
            finish(h, h)

            @pl.when(tm > 0)
            def _():
                path_copy(h).start()

            ncur[h, PAD - 1 : PAD, :] = cur[h, PAD + T - 1 : PAD + T, :]
            curve(h, [0], T, linear_of(h, [0], T), drive[h].reshape(T, U))

        compose(h, g)

        @pl.when(g == NG - 1)
        def _():
            close_slab(h, sweep * 2 + h)

        return carry

    lax.fori_loop(0, 16, unit_step, 0)

    def out_copy(h):
        return pltpu.make_async_copy(
            cur.at[h, pl.ds(PAD, T)], traj_ref.at[:, pl.ds(h * U, U)], local_sem.at[h]
        )

    def next_copy(h):
        return pltpu.make_async_copy(
            ahead.at[h], next_ref.at[:, pl.ds(h * U, U)], local_sem.at[2 + h]
        )

    def follow(h):
        @pl.when(tm < NX * NY - 1)
        def _():
            start_copy(h).wait_recv()
            advance(h, norigin[h], nslope, noffset, ahead, 0)

        @pl.when(tm == NX * NY - 1)
        def _():
            ahead[h] = jnp.broadcast_to(cur[h, PAD + T - 1 : PAD + T, :], (T, U))

        next_copy(h).start()

    finish(0, 2, last=True)
    out_copy(0).start()

    def following_curve():
        @pl.when(tm < NX * NY - 1)
        def _():
            for g in range(NG):
                drive_copy(g).wait_recv()
            for h in range(2):
                path_copy(h).wait_recv()
                linear = linear_of(h, [0], T, ncur)
                curve(h, [0], T, linear, ndrive[h].reshape(T, U), nslope, noffset)

    close_row(3)

    @pl.when(my_y > 0)
    def _():
        following_curve()

    @pl.when(my_y >= 2)
    def _():
        follow(0)

    for y in range(NY - 1):
        pass_row(1, 3, y)

    @pl.when(my_y == 0)
    def _():
        following_curve()

    @pl.when(my_y < 2)
    def _():
        follow(0)

    state = begin(1, 3, last=True)
    half_way = L // 2
    for step in range(half_way):
        state = advance_step(1, state, step, slope, offset, cur, PAD)

    @pl.when(tm < NX * NY - 1)
    def _():
        start_copy(1).wait_recv()
        own, following = state, norigin[1]
        for step in range(L):
            following = advance_step(1, following, step, nslope, noffset, ahead, 0)
            if half_way + step < L:
                own = advance_step(1, own, half_way + step, slope, offset, cur, PAD)

    @pl.when(tm == NX * NY - 1)
    def _():
        own = state
        for step in range(half_way, L):
            own = advance_step(1, own, step, slope, offset, cur, PAD)
        ahead[1] = jnp.broadcast_to(cur[1, PAD + T - 1 : PAD + T, :], (T, U))

    out_copy(1).start()
    next_copy(1).start()

    def drain(g, carry):
        for kind, to in ((0, ahead_z), (1, back_z), (2, partner)):
            own_chunk(g, kind, to).wait_send()
        held_chunk(g, 3, back_z, ahead_z).wait_send()
        held_chunk(g, 6, back_z, across).wait_send()
        for kind, source in ((4, back_z), (5, ahead_z)):
            held_chunk(g, kind, source, partner).wait_send()
        return carry

    lax.fori_loop(0, NG, drain, 0)

    @pl.when(tm < NX * NY - 1)
    def _():
        edge_copy.wait_send()

    for unit in range(4):
        for k in range(1, NX):
            row_copy(unit, k).wait_send()

        @pl.when(my_y < NY - 1)
        def _():
            state_copy(unit, my_y).wait_send()

    @pl.when(tm > 0)
    def _():
        for g in range(NG):
            drive_copy(g).wait_send()
        for h in range(2):
            start_copy(h).wait_send()

    for h in range(2):
        out_copy(h).wait()
        next_copy(h).wait()


def shards(inputs, in_weight, rec_weight, bias, initial, guess):
    hbm = pl.BlockSpec(memory_space=pltpu.HBM)
    anywhere = pl.BlockSpec(memory_space=pl.ANY)
    out = jax.ShapeDtypeStruct((T, 2 * U), F32)
    dma = pltpu.SemaphoreType.DMA
    results = pl.pallas_call(
        kernel,
        out_shape=(out, out),
        in_specs=[hbm] * 6,
        out_specs=(anywhere, anywhere),
        scratch_shapes=[
            pltpu.VMEM((2, U, U), F32),
            pltpu.VMEM((2, U), F32),
            pltpu.VMEM((2, U), F32),
            pltpu.VMEM((2 * NZ, NB, S, 2 * U), BF16),
            pltpu.VMEM((2 * NZ * 2 * U, 2 * U), BF16),
            pltpu.VMEM((2, 2 * U, 2 * U), BF16),
            pltpu.VMEM((2, PAD + T, U), F32),
            pltpu.VMEM((2, NB, S, U), F32),
            pltpu.VMEM((2, T, U), F32),
            pltpu.VMEM((2, T, U), F32),
            pltpu.VMEM((NB, U, 2 * U), BF16),
            pltpu.VMEM((2, NG + 1, NB, M, 2 * U), BF16),
            pltpu.VMEM((2, 4, M, 2 * U), BF16),
            pltpu.VMEM((2, 2, M, 2 * U), BF16),
            pltpu.VMEM((2, NB, U), F32),
            pltpu.VMEM((4, NX, M, 2 * U), BF16),
            pltpu.VMEM((M, 2 * U), BF16),
            pltpu.VMEM((4, 16, U), F32),
            pltpu.VMEM((4, 16, U), F32),
            pltpu.VMEM((2, M, 2 * U), BF16),
            pltpu.VMEM((8, 2 * U), F32),
            pltpu.VMEM((16, U), F32),
            pltpu.VMEM((2, NB, S, U), F32),
            pltpu.VMEM((2, PAD + T, U), F32),
            pltpu.VMEM((2, T, U), F32),
            pltpu.VMEM((2, T, U), F32),
            pltpu.VMEM((2, B, U), F32),
            pltpu.VMEM((2, B, U), F32),
            pltpu.VMEM((2, T, U), F32),
            dma((7,)),
            dma((7, NG)),
            dma((2 * NZ, NG)),
            dma((4, NX)),
            dma((4, NX)),
            dma((4,)),
            dma((4,)),
            dma((1,)),
            dma((1,)),
            dma((2,)),
            dma((2,)),
            dma((NG,)),
            dma((NG,)),
            dma((2,)),
            dma((2,)),
        ],
        compiler_params=pltpu.CompilerParams(
            collective_id=0, has_side_effects=True, vmem_limit_bytes=56 * 1024 * 1024
        ),
    )(
        inputs.reshape(NB, S, 2 * U),
        in_weight,
        rec_weight,
        bias.reshape(2, U),
        initial.reshape(2, U),
        guess,
    )
    return pl.pallas_call(
        emit,
        out_shape=(out, out),
        in_specs=[anywhere] * 2,
        out_specs=(anywhere, anywhere),
        scratch_shapes=[pltpu.VMEM((2, T, 2 * U), F32), dma((4,)), dma((4,))],
    )(*results)


def emit(a_ref, b_ref, out_a, out_b, held, in_sem, out_sem):
    half = T // 2
    parts = [(k, pl.ds(half * i, half)) for k in range(2) for i in range(2)]
    pairs = ((a_ref, out_a), (b_ref, out_b))
    ins = [
        pltpu.make_async_copy(pairs[k][0].at[rows], held.at[k, rows], in_sem.at[n])
        for n, (k, rows) in enumerate(parts)
    ]
    outs = [
        pltpu.make_async_copy(held.at[k, rows], pairs[k][1].at[rows], out_sem.at[n])
        for n, (k, rows) in enumerate(parts)
    ]
    for copy in ins:
        copy.start()
    for arriving, leaving in zip(ins, outs):
        arriving.wait()
        leaving.start()
    for copy in outs:
        copy.wait()


def solution(mesh):
    in_specs = (
        P("tm", "head"),
        P(None, "head"),
        P("head", None, None),
        P("head"),
        P("head"),
        P("tm", "head"),
    )
    out_specs = (P("tm", "head"), P("tm", "head"))
    return jax.shard_map(
        shards, mesh=mesh, in_specs=in_specs, out_specs=out_specs, check_vma=False
    )
```
